128 devices in a mesh: grp: 2 (over y_lo), orb: 64 (over y_hi, z, x, core).
Axes of the slice: x: 4, y: 4 (y_hi: 2, y_lo: 2; y = y_hi * 2 + y_lo), z: 4, core: 2. Of those that a mesh axis runs over, the one named last changes fastest.
Arguments:
- occupied: float32 [64, 262144], P('orb'), may hold values from -5 to 5
- targets: float32 [128, 262144], P(('grp', 'orb')), may hold values from -8 to 8
- potential: float32 [262144], P('orb'), may hold values from -4 to 4
Outputs:
- updated: float32 [128, 262144], P('grp', 'orb')
The draws below stay inside these ranges and needn't reach their ends.
All inputs are finite; a program needn't handle non-finite values.
Results may differ from the reference program's by a relative error of at most 0.0003.
Values sent between devices are 32-bit elements; how exact they have to be, the bound alone decides.
A program may use at most 64 MiB of HBM per device.

```python
import jax
import jax.numpy as jnp
from jax import lax

NGRID = 64
CELLS = 262144
TGT_DEV = 1
OCC_DEV = 1
CYCLE = 2
INNER = 1
NT = 128
NOCC = 64
N_GRP = 2
N_ORB = 64


def draw_targets(key, part):
    first_key, second_key = jax.random.split(jax.random.fold_in(key, 11), 2)
    common = jnp.clip(jax.random.normal(second_key, (1, CELLS), jnp.float32), -5.0, 5.0)
    rough = jnp.clip(jax.random.normal(first_key, (NT, CELLS), jnp.float32), -5.0, 5.0)
    return rough + 0.6 * common


def levels(stream_key, shape, cuts, low, high):
    gain, own = 1.0, jax.random.fold_in(stream_key, 6)
    for dim, parts in cuts:
        heights = jnp.exp(jax.random.uniform(jax.random.fold_in(own, dim), (parts,), jnp.float32, low / len(cuts), high / len(cuts)))
        gain = gain * jnp.repeat(heights, shape[dim] // parts).reshape([-1 if axis == dim else 1 for axis in range(len(shape))])
    return gain


def scatter_about(key, dims, scale, limit, cuts=(), kind=jnp.bfloat16):
    gain = levels(key, dims, cuts, -0.22, 0.18) if cuts else 1.0
    drawn = jax.random.normal(key, dims, jnp.float32) * scale * gain
    return jnp.minimum(jnp.maximum(drawn, -limit), limit).astype(kind)


def setup_inputs(seed: int = 0) -> dict:
    seeds = jax.random.split(jax.random.key(seed), 4)
    return {
        "occupied": scatter_about(seeds[0], (NOCC, CELLS), 1.0, 5.0, ((0, 64),), jnp.float32),
        "targets": draw_targets(jax.random.fold_in(seeds[3], 71), 0),
        "potential": scatter_about(seeds[2], (CELLS,), 1.0, 4.0, ((0, 64),), jnp.float32),
    }


SCREEN_SQ = 0.04
BOX_LENGTH = 20.0
STEP_SIZE = 0.3

def kernel_cube():
    points = NGRID
    index = jnp.arange(points, dtype=jnp.int32)
    folded = jnp.minimum(index, points - index).astype(jnp.float32) * (2.0 * jnp.pi / BOX_LENGTH)
    squared = folded * folded
    total_sq = squared[:, None, None] + squared[None, :, None] + squared[None, None, :]
    return 4.0 * jnp.pi / (total_sq + SCREEN_SQ)

def coulomb_solve(fields):
    points = NGRID
    cube = fields.reshape(-1, points, points, points)
    spectrum = jnp.fft.rfftn(cube, axes=(1, 2, 3))
    kernel = kernel_cube()[:, :, :points // 2 + 1]
    solved = jnp.fft.irfftn(spectrum * kernel, s=(points, points, points), axes=(1, 2, 3))
    return solved.reshape(fields.shape)

def exchange_rows(position, occupied, targets):
    rows = lax.dynamic_slice_in_dim(targets, position * TGT_DEV, TGT_DEV, 0)
    center = position % N_ORB
    offsets = jnp.arange(-CYCLE, CYCLE + 1, dtype=jnp.int32)
    blocks = (center + offsets) % N_ORB
    row_ids = (blocks[:, None] * OCC_DEV + jnp.arange(OCC_DEV, dtype=jnp.int32)[None, :]).reshape(-1)
    nearby = jnp.take(occupied, row_ids, axis=0)
    products = (rows[:, None, :] * nearby[None, :, :]).reshape(-1, CELLS)
    solved = coulomb_solve(products).reshape(TGT_DEV, -1, CELLS)
    return -jnp.sum(nearby[None] * solved, axis=1)

def gram(left, right):
    inner = lax.dot_general(left, right, (((1,), (1,)), ((), ())), precision=lax.Precision.HIGHEST)
    return inner / CELLS

def reference(occupied, targets, potential):
    positions = jnp.arange(N_GRP * N_ORB, dtype=jnp.int32)
    exchange = lax.map(lambda position: exchange_rows(position, occupied, targets), positions).reshape(NT, CELLS)
    correlation = gram(exchange, exchange)
    factor = jnp.linalg.cholesky(correlation)
    compressed = lax.linalg.triangular_solve(factor, exchange, left_side=True, lower=True)
    current = targets
    for repeat in range(INNER):
        projection = gram(current, compressed)
        applied = potential[None, :] * current - jnp.dot(projection, compressed, precision=lax.Precision.HIGHEST)
        rayleigh = gram(applied, current)
        current = current - STEP_SIZE * (applied - jnp.dot(rayleigh, current, precision=lax.Precision.HIGHEST))
    return current
```

```python
import functools
import ml_dtypes
import jax
import jax.numpy as jnp
from jax.sharding import PartitionSpec as P
from jax import lax
from jax.experimental import pallas as pl
from jax.experimental.pallas import tpu as pltpu
import numpy as np
NG=64; CELLS=262144
SCREEN_SQ=0.04; BOX_LENGTH=20.0
BF=jnp.bfloat16; F32=jnp.float32

def tables():
    bf=ml_dtypes.bfloat16
    i=np.arange(64)
    ang=2*np.pi*((i[:,None]*i[None,:])%64)/64
    H=(np.cos(ang)+np.sin(ang)).astype(np.float32)
    Hh=H.astype(bf); Hl=(H-Hh.astype(np.float32)).astype(bf)
    perm=2*(i%32)+i//32
    ax=np.concatenate([Hh,Hh,Hl],1)
    ay=ax.reshape(64,3,64)[perm][:,:,perm].reshape(64,192)
    z=np.zeros((64,64),bf)
    bd=lambda m: np.block([[m,z],[z,m]])
    row=np.concatenate([bd(Hh),bd(Hl)],1)
    wz=np.concatenate([row,row],0)
    ind=jnp.arange(64); q=jnp.minimum(ind,64-ind).astype(F32)*(2*jnp.pi/BOX_LENGTH); q2=q*q
    qb=q2.reshape(32,2).T
    tot=qb.T[:,None,:,None]+q2[None,:,None,None]+q2[None,None,None,:]
    K=(4*jnp.pi/(tot+SCREEN_SQ))*(1.0/CELLS)
    return jnp.asarray(ax),jnp.asarray(ay),jnp.asarray(wz),K.reshape(2048,128)

def split(x):
    h=x.astype(BF); l=(x-h.astype(F32)).astype(BF)
    return h,l
def dot(a,b): return jnp.dot(a,b,preferred_element_type=F32)

def swap(lo,hi,mask):
    return jnp.where(mask,lo,pltpu.roll(hi,64,1)), jnp.where(mask,pltpu.roll(lo,64,1),hi)

def left(A,planes):
    out=[]
    for k in range(0,len(planes),2):
        d=jnp.concatenate(planes[k:k+2],1)
        h,l=split(d)
        r=dot(A,jnp.concatenate([h,l,h],0))
        out+= [r[:,:128],r[:,128:]]
    return out
def zt(x,W):
    h,l=split(x)
    r=dot(jnp.concatenate([h,l],1),W)
    return r[:,:128]+r[:,128:]

def fwd_chunk(prod,ay,wz,mask,P):
    b=[]
    for p in range(P):
        u,v=swap(prod[2*p],prod[2*p+1],mask); b+=[u,v]
    x=zt(jnp.concatenate(b,0),wz)
    pl_=left(ay,[x[64*p:64*p+64] for p in range(P)])
    out=[]
    for p in range(P):
        u,v=swap(pl_[p][:32],pl_[p][32:],mask); out+=[u,v]
    return out

def kernel(P,R,t_ref,o_ref,ein_ref,ax_ref,ay_ref,wz_ref,k_ref,e_ref,s_ref):
    mask=lax.broadcasted_iota(jnp.int32,(32,128),1)<64
    ax=ax_ref[...];ay=ay_ref[...];wz=wz_ref[...]
    n=64*P
    def fwd(i,c):
        base=pl.multiple_of(i*n,n)
        pr=t_ref[pl.ds(base,n),:]*o_ref[pl.ds(base,n),:]
        out=fwd_chunk([pr[32*k:32*k+32] for k in range(2*P)],ay,wz,mask,P)
        s_ref[pl.ds(base,n),:]=jnp.concatenate(out,0)
        return c
    lax.fori_loop(0,32//P,fwd,0)
    def mid(i,c):
        pls=[s_ref[pl.ds(i*R+r,64,stride=32),:] for r in range(R)]
        f=left(ax,pls)
        kk=k_ref[pl.ds(pl.multiple_of(i*R*64,R*64),R*64),:]
        f=[f[r]*kk[64*r:64*r+64] for r in range(R)]
        f=left(ax,f)
        for r in range(R): s_ref[pl.ds(i*R+r,64,stride=32),:]=f[r]
        return c
    lax.fori_loop(0,32//R,mid,0)
    def inv(i,c):
        base=pl.multiple_of(i*n,n)
        sv=s_ref[pl.ds(base,n),:]
        b=[]
        for p in range(P):
            u,v=swap(sv[64*p:64*p+32],sv[64*p+32:64*p+64],mask)
            b.append(jnp.concatenate([u,v],0))
        x=zt(jnp.concatenate(left(ay,b),0),wz)
        out=[]
        for p in range(P):
            u,v=swap(x[64*p:64*p+32],x[64*p+32:64*p+64],mask); out+=[u,v]
        e_ref[pl.ds(base,n),:]=ein_ref[pl.ds(base,n),:]-jnp.concatenate(out,0)*o_ref[pl.ds(base,n),:]
        return c
    lax.fori_loop(0,32//P,inv,0)


STEP_SIZE = 0.3
CYCLE = 2
PLANES, ROWS = 16, 16


def solve_call(t, o, ein, tabs):
    vm = pl.BlockSpec(memory_space=pltpu.VMEM)
    return pl.pallas_call(
        functools.partial(kernel, PLANES, ROWS),
        out_shape=jax.ShapeDtypeStruct((2048, 128), F32),
        in_specs=[vm] * 7,
        out_specs=vm,
        scratch_shapes=[pltpu.VMEM((2048, 128), F32)],
        compiler_params=pltpu.CompilerParams(vmem_limit_bytes=32 << 20),
        cost_estimate=pl.CostEstimate(flops=2000000000, bytes_accessed=5 << 20, transcendentals=0),
    )(t, o, ein, *tabs)


def shifted(x, axis, by):
    size = lax.axis_size(axis)
    return lax.ppermute(x, axis, [(i, (i + by) % size) for i in range(size)])


def swapped(x, axis):
    return lax.ppermute(x, axis, [(0, 1), (1, 0)])


HI = lax.Precision.HIGHEST


def mm(a, b):
    return jnp.dot(a, b, precision=HI)


def mmt(a, b):
    return lax.dot_general(a, b, (((1,), (1,)), ((), ())), precision=HI)


def to_cells(row):
    pieces = row.reshape(64, 2, 2048).transpose(1, 0, 2).reshape(128, 2048)
    return lax.all_to_all(pieces, ("grp", "orb"), split_axis=0, concat_axis=0, tiled=True)


def on_device(occupied, targets, potential):
    g = lax.axis_index("grp")
    tabs = tables()
    t = targets.reshape(2048, 128)
    up = [occupied]
    down = [occupied]
    for repeat in range(CYCLE):
        up.append(shifted(up[-1], "orb", 1))
        down.append(shifted(down[-1], "orb", -1))
    e = jnp.zeros((2048, 128), F32)
    for visiting in (occupied, up[1], down[1], up[2], down[2]):
        e = solve_call(t, visiting.reshape(2048, 128), e, tabs)
    T = to_cells(targets)
    E = to_cells(e)
    v = lax.dynamic_slice_in_dim(potential, g * 2048, 2048, 0)
    VT = v[None, :] * T
    grams = jnp.concatenate([mmt(E, E), mmt(T, E), mmt(VT, T)], 0) / CELLS
    grams = lax.psum(grams, ("grp", "orb"))
    gee, gte, gvt = grams[:128], grams[128:256], grams[256:]
    factor = jnp.linalg.cholesky(gee)
    half = lax.linalg.triangular_solve(factor, gte.T, left_side=True, lower=True)
    mt = lax.linalg.triangular_solve(factor, half, left_side=True, lower=True, transpose_a=True)
    ray = gvt - mm(half.T, half)
    coeff = jnp.concatenate([mt.T, ray], 1)
    both = jnp.concatenate([E, T], 0)

    def rows_of(which):
        c = lax.dynamic_slice_in_dim(coeff, which * 64, 64, 0)
        old = lax.dynamic_slice_in_dim(T, which * 64, 64, 0)
        return old - STEP_SIZE * (v[None, :] * old - mm(c, both))

    theirs = rows_of(1 - g)
    received = swapped(theirs, "grp")
    mine = rows_of(g)
    return jnp.where(g == 0, jnp.concatenate([mine, received], 1), jnp.concatenate([received, mine], 1))


def solution(mesh):
    placed = (P("orb", None), P(("grp", "orb"), None), P("orb"))
    return jax.shard_map(
        on_device, mesh=mesh, in_specs=placed, out_specs=P("grp", "orb"), check_vma=False
    )
```

```python
import functools
import ml_dtypes
import jax
import jax.numpy as jnp
from jax.sharding import PartitionSpec as P
from jax import lax
from jax.experimental import pallas as pl
from jax.experimental.pallas import tpu as pltpu
import numpy as np
NG=64; CELLS=262144
SCREEN_SQ=0.04; BOX_LENGTH=20.0
BF=jnp.bfloat16; F32=jnp.float32

def tables():
    bf=ml_dtypes.bfloat16
    i=np.arange(64)
    ang=2*np.pi*((i[:,None]*i[None,:])%64)/64
    H=(np.cos(ang)+np.sin(ang)).astype(np.float32)
    Hh=H.astype(bf); Hl=(H-Hh.astype(np.float32)).astype(bf)
    perm=2*(i%32)+i//32
    ax=np.concatenate([Hh,Hh,Hl],1)
    ay=ax.reshape(64,3,64)[perm][:,:,perm].reshape(64,192)
    z=np.zeros((64,64),bf)
    bd=lambda m: np.block([[m,z],[z,m]])
    row=np.concatenate([bd(Hh),bd(Hl)],1)
    wz=np.concatenate([row,row],0)
    ind=jnp.arange(64); q=jnp.minimum(ind,64-ind).astype(F32)*(2*jnp.pi/BOX_LENGTH); q2=q*q
    qb=q2.reshape(32,2).T
    tot=qb.T[:,None,:,None]+q2[None,:,None,None]+q2[None,None,None,:]
    K=(4*jnp.pi/(tot+SCREEN_SQ))*(1.0/CELLS)
    return jnp.asarray(ax),jnp.asarray(ay),jnp.asarray(wz),K.reshape(2048,128)

def split(x):
    h=x.astype(BF); l=(x-h.astype(F32)).astype(BF)
    return h,l
def dot(a,b): return jnp.dot(a,b,preferred_element_type=F32)

def swap(lo,hi,mask):
    return jnp.where(mask,lo,pltpu.roll(hi,64,1)), jnp.where(mask,pltpu.roll(lo,64,1),hi)

def left(A,planes):
    out=[]
    for k in range(0,len(planes),2):
        d=jnp.concatenate(planes[k:k+2],1)
        h,l=split(d)
        r=dot(A,jnp.concatenate([h,l,h],0))
        out+= [r[:,:128],r[:,128:]]
    return out
def zt(x,W):
    h,l=split(x)
    r=dot(jnp.concatenate([h,l],1),W)
    return r[:,:128]+r[:,128:]

def fwd_chunk(prod,ay,wz,mask,P):
    b=[]
    for p in range(P):
        u,v=swap(prod[2*p],prod[2*p+1],mask); b+=[u,v]
    x=zt(jnp.concatenate(b,0),wz)
    pl_=left(ay,[x[64*p:64*p+64] for p in range(P)])
    out=[]
    for p in range(P):
        u,v=swap(pl_[p][:32],pl_[p][32:],mask); out+=[u,v]
    return out

def kernel(P,R,t_ref,o_ref,ein_ref,ax_ref,ay_ref,wz_ref,k_ref,e_ref,s_ref):
    mask=lax.broadcasted_iota(jnp.int32,(32,128),1)<64
    ax=ax_ref[...];ay=ay_ref[...];wz=wz_ref[...]
    n=64*P
    def fwd(i,c):
        base=pl.multiple_of(i*n,n)
        pr=t_ref[pl.ds(base,n),:]*o_ref[pl.ds(base,n),:]
        out=fwd_chunk([pr[32*k:32*k+32] for k in range(2*P)],ay,wz,mask,P)
        s_ref[pl.ds(base,n),:]=jnp.concatenate(out,0)
        return c
    lax.fori_loop(0,32//P,fwd,0)
    def mid(i,c):
        pls=[s_ref[pl.ds(i*R+r,64,stride=32),:] for r in range(R)]
        f=left(ax,pls)
        kk=k_ref[pl.ds(pl.multiple_of(i*R*64,R*64),R*64),:]
        f=[f[r]*kk[64*r:64*r+64] for r in range(R)]
        f=left(ax,f)
        for r in range(R): s_ref[pl.ds(i*R+r,64,stride=32),:]=f[r]
        return c
    lax.fori_loop(0,32//R,mid,0)
    def inv(i,c):
        base=pl.multiple_of(i*n,n)
        sv=s_ref[pl.ds(base,n),:]
        b=[]
        for p in range(P):
            u,v=swap(sv[64*p:64*p+32],sv[64*p+32:64*p+64],mask)
            b.append(jnp.concatenate([u,v],0))
        x=zt(jnp.concatenate(left(ay,b),0),wz)
        out=[]
        for p in range(P):
            u,v=swap(x[64*p:64*p+32],x[64*p+32:64*p+64],mask); out+=[u,v]
        e_ref[pl.ds(base,n),:]=ein_ref[pl.ds(base,n),:]-jnp.concatenate(out,0)*o_ref[pl.ds(base,n),:]
        return c
    lax.fori_loop(0,32//P,inv,0)


MESH=pl.DeviceIdType.MESH
def home(k):
    o=2*(k%32)
    g=(k//32+k%32+(k%32)//4+(k%32)//16)%2
    return g,o
def ar_kernel(n, x_ref, out_ref, parts, sums, ssem, rsem, gsem, hsem):
    g=lax.axis_index("grp"); o=lax.axis_index("orb")
    me=g*64+o
    bar=pltpu.get_barrier_semaphore()
    def sig(k,c):
        d=lax.rem(me+k,128)
        pl.semaphore_signal(bar,inc=1,device_id=(d//64,lax.rem(d,64)),device_id_type=MESH)
        return c
    lax.fori_loop(1,128,sig,0)
    pl.semaphore_wait(bar,127)
    def tile_of(k):
        hg,ho=home(k)
        return hg,ho,(hg==g)&(ho==o)
    def send(k,c):
        hg,ho,mine=tile_of(k)
        src=x_ref.at[pl.ds(pl.multiple_of(k*8,8),8),:]
        @pl.when(mine)
        def _(): pltpu.make_async_copy(src,parts.at[me],rsem).start()
        @pl.when(jnp.logical_not(mine))
        def _(): pltpu.make_async_remote_copy(src_ref=src,dst_ref=parts.at[me],send_sem=ssem,recv_sem=rsem,device_id=(hg,ho),device_id_type=MESH).start()
        return c
    lax.fori_loop(0,n,send,0)
    def work(k,c):
        hg,ho,mine=tile_of(k)
        @pl.when(mine)
        def _():
            pltpu.make_async_copy(parts,parts,rsem).wait()
            sums[...]=jnp.sum(parts[...],axis=0)
            dst=out_ref.at[pl.ds(pl.multiple_of(k*8,8),8),:]
            pltpu.make_async_copy(sums,dst,hsem).start()
            def bc(j,c2):
                d=lax.rem(me+j,128)
                pltpu.make_async_remote_copy(src_ref=sums,dst_ref=dst,send_sem=gsem,recv_sem=hsem,device_id=(d//64,lax.rem(d,64)),device_id_type=MESH).start()
                return c2
            lax.fori_loop(1,128,bc,0)
        return c
    lax.fori_loop(0,n,work,0)
    pltpu.make_async_copy(out_ref,out_ref,hsem).wait()
    def drain(k,c):
        hg,ho,mine=tile_of(k)
        @pl.when(jnp.logical_not(mine))
        def _():
            pltpu.make_async_copy(sums,sums,ssem).wait()
        @pl.when(mine)
        def _():
            pltpu.make_async_copy(parts.at[pl.ds(0,127)],parts.at[pl.ds(0,127)],gsem).wait()
        return c
    lax.fori_loop(0,n,drain,0)
def all_reduce(x, cid=0):
    n=x.shape[0]//8
    vm=pl.BlockSpec(memory_space=pltpu.VMEM)
    return pl.pallas_call(functools.partial(ar_kernel,n),out_shape=jax.ShapeDtypeStruct(x.shape,F32),
      in_specs=[vm],out_specs=vm,
      scratch_shapes=[pltpu.VMEM((128,8,128),F32),pltpu.VMEM((8,128),F32)]+[pltpu.SemaphoreType.DMA]*4,
      compiler_params=pltpu.CompilerParams(collective_id=cid,has_side_effects=True))(x)


STEP_SIZE = 0.3
CYCLE = 2
PLANES, ROWS = 16, 16


def solve_call(t, o, ein, tabs):
    vm = pl.BlockSpec(memory_space=pltpu.VMEM)
    return pl.pallas_call(
        functools.partial(kernel, PLANES, ROWS),
        out_shape=jax.ShapeDtypeStruct((2048, 128), F32),
        in_specs=[vm] * 7,
        out_specs=vm,
        scratch_shapes=[pltpu.VMEM((2048, 128), F32)],
        compiler_params=pltpu.CompilerParams(vmem_limit_bytes=32 << 20),
        cost_estimate=pl.CostEstimate(flops=2000000000, bytes_accessed=5 << 20, transcendentals=0),
    )(t, o, ein, *tabs)


def shifted(x, axis, by):
    size = lax.axis_size(axis)
    return lax.ppermute(x, axis, [(i, (i + by) % size) for i in range(size)])


def swapped(x, axis):
    return lax.ppermute(x, axis, [(0, 1), (1, 0)])


HI = lax.Precision.HIGHEST


def mm(a, b):
    return jnp.dot(a, b, precision=HI)


def mmt(a, b):
    return lax.dot_general(a, b, (((1,), (1,)), ((), ())), precision=HI)


def to_cells(row):
    pieces = row.reshape(64, 2, 2048).transpose(1, 0, 2).reshape(128, 2048)
    return lax.all_to_all(pieces, ("grp", "orb"), split_axis=0, concat_axis=0, tiled=True)


def on_device(occupied, targets, potential):
    g = lax.axis_index("grp")
    tabs = tables()
    t = targets.reshape(2048, 128)
    up = [occupied]
    down = [occupied]
    for repeat in range(CYCLE):
        up.append(shifted(up[-1], "orb", 1))
        down.append(shifted(down[-1], "orb", -1))
    e = jnp.zeros((2048, 128), F32)
    for visiting in (occupied, up[1], down[1], up[2], down[2]):
        e = solve_call(t, visiting.reshape(2048, 128), e, tabs)
    T = to_cells(targets)
    E = to_cells(e)
    v = lax.dynamic_slice_in_dim(potential, g * 2048, 2048, 0)
    VT = v[None, :] * T
    grams = jnp.concatenate([mmt(E, E), mmt(T, E), mmt(VT, T)], 0) / CELLS
    grams = all_reduce(grams)
    gee, gte, gvt = grams[:128], grams[128:256], grams[256:]
    factor = jnp.linalg.cholesky(gee)
    half = lax.linalg.triangular_solve(factor, gte.T, left_side=True, lower=True)
    mt = lax.linalg.triangular_solve(factor, half, left_side=True, lower=True, transpose_a=True)
    ray = gvt - mm(half.T, half)
    coeff = jnp.concatenate([mt.T, ray], 1)
    both = jnp.concatenate([E, T], 0)

    def rows_of(which):
        c = lax.dynamic_slice_in_dim(coeff, which * 64, 64, 0)
        old = lax.dynamic_slice_in_dim(T, which * 64, 64, 0)
        return old - STEP_SIZE * (v[None, :] * old - mm(c, both))

    theirs = rows_of(1 - g)
    received = swapped(theirs, "grp")
    mine = rows_of(g)
    return jnp.where(g == 0, jnp.concatenate([mine, received], 1), jnp.concatenate([received, mine], 1))


def solution(mesh):
    placed = (P("orb", None), P(("grp", "orb"), None), P("orb"))
    return jax.shard_map(
        on_device, mesh=mesh, in_specs=placed, out_specs=P("grp", "orb"), check_vma=False
    )
```

```python
import functools
import ml_dtypes
import jax
import jax.numpy as jnp
from jax.sharding import PartitionSpec as P
from jax import lax
from jax.experimental import pallas as pl
from jax.experimental.pallas import tpu as pltpu
import numpy as np
BF=jnp.bfloat16; F32=jnp.float32
MESH=pl.DeviceIdType.MESH
CELLS=262144
NDEV=128
CH=4
CP=32//CH
CR=2048//CH

def tables():
    bf=ml_dtypes.bfloat16
    i=np.arange(64)
    ang=2*np.pi*((i[:,None]*i[None,:])%64)/64
    H=(np.cos(ang)+np.sin(ang)).astype(np.float32)
    Hh=H.astype(bf); Hl=(H-Hh.astype(np.float32)).astype(bf)
    perm=2*(i%32)+i//32
    ax=np.concatenate([Hh,Hh,Hl],1)
    ay=ax.reshape(64,3,64)[perm][:,:,perm].reshape(64,192)
    z=np.zeros((64,64),bf)
    bd=lambda m: np.block([[m,z],[z,m]])
    row=np.concatenate([bd(Hh),bd(Hl)],1)
    wz=np.concatenate([row,row],0)
    q=np.minimum(i,64-i).astype(np.float32)*np.float32(2*np.pi/20.0); q2=q*q
    qa=np.broadcast_to((q2+np.float32(0.04))[:,None],(64,128))
    qb=q2.reshape(32,2)
    qr=(qb[:,:,None]+q2[None,None,:]).reshape(32,128)
    return ax,ay,wz,np.concatenate([qa,qr],0).astype(np.float32)

def split(x):
    h=x.astype(BF)
    return h,(x-h.astype(F32)).astype(BF)
def dot(a,b): return jnp.dot(a,b,preferred_element_type=F32)
def half_swap(lo,hi,mask):
    return jnp.where(mask,lo,pltpu.roll(hi,64,1)), jnp.where(mask,pltpu.roll(lo,64,1),hi)
def left(A,planes):
    out=[]
    for k in range(0,len(planes),2):
        h,l=split(jnp.concatenate(planes[k:k+2],1))
        r=dot(A,jnp.concatenate([h,l,h],0))
        out+=[r[:,:128],r[:,128:]]
    return out
def lanes(x,W):
    h,l=split(x)
    r=dot(jnp.concatenate([h,l],1),W)
    return r[:,:128]+r[:,128:]

def peer(d): return (d//64,lax.rem(d,64))

def k1(t_ref,o_ref,ax_ref,ay_ref,wz_ref,q_ref,tc,ec,ob,sb,kt,e,osend,arecv,brecv,crecv,drecv,tsend,trecv,esend,erecv,loc):
    g=lax.axis_index("grp"); o=lax.axis_index("orb"); me=g*64+o
    s=2*lax.rem(o,2)-1
    w=lambda v: lax.rem(v+128,64)
    inner=(g,w(o-s)); outer=(g,w(o+s)); across=(g,w(o-2*s))
    bar=pltpu.get_barrier_semaphore()
    def sig(k,c):
        pl.semaphore_signal(bar,inc=1,device_id=peer(lax.rem(me+k,NDEV)),device_id_type=MESH)
        return c
    lax.fori_loop(1,NDEV,sig,0)
    own=pltpu.make_async_copy(o_ref,ob.at[0],loc); own.start()
    mask=lax.broadcasted_iota(jnp.int32,(32,128),1)<64
    ax=ax_ref[...];ay=ay_ref[...];wz=wz_ref[...]
    qa=q_ref[0:64,:]
    def ktab(r,c):
        kt[pl.ds(pl.multiple_of(r*64,64),64),:]=(4*np.pi/CELLS)/(qa+q_ref[pl.ds(64+r,1),:])
        return c
    lax.fori_loop(0,32,ktab,0,unroll=8)
    own.wait()
    def rows(q): return pl.ds(pl.multiple_of(q*CR,CR),CR)
    def fwd(j,q):
        pr=t_ref[rows(q),:]*ob[j,rows(q),:]
        b=[]
        for p in range(CP):
            b+=half_swap(pr[64*p:64*p+32],pr[64*p+32:64*p+64],mask)
        x=lanes(jnp.concatenate(b,0),wz)
        f=left(ay,[x[64*p:64*p+64] for p in range(CP)])
        out=[]
        for p in range(CP): out+=half_swap(f[p][:32],f[p][32:],mask)
        sb[j,rows(q),:]=jnp.concatenate(out,0)
    R=16
    def mid(j):
        def half(i,c):
            f=left(ax,[sb[j,pl.ds(i*R+r,64,stride=32),:] for r in range(R)])
            kk=kt[pl.ds(pl.multiple_of(i*R*64,R*64),R*64),:]
            f=left(ax,[f[r]*kk[64*r:64*r+64] for r in range(R)])
            for r in range(R): sb[j,pl.ds(i*R+r,64,stride=32),:]=f[r]
            return c
        lax.fori_loop(0,32//R,half,0)
    def inv(js,q,first):
        b=[]
        for j in js:
            sv=sb[j,rows(q),:]
            for p in range(CP):
                u,v=half_swap(sv[64*p:64*p+32],sv[64*p+32:64*p+64],mask)
                b.append(jnp.concatenate([u,v],0))
        x=lanes(jnp.concatenate(left(ay,b),0),wz)
        acc=None if first else e[rows(q),:]
        for n,j in enumerate(js):
            out=[]
            for p in range(CP):
                k=64*(n*CP+p)
                out+=half_swap(x[k:k+32],x[k+32:k+64],mask)
            term=jnp.concatenate(out,0)*ob[j,rows(q),:]
            acc=-term if acc is None else acc-term
        e[rows(q),:]=acc
    def chunks(f):
        def body(q,c):
            f(q)
            return c
        lax.fori_loop(0,CH,body,0)
    def push(dst_dev,slot,q,rsem,src):
        return pltpu.make_async_remote_copy(src_ref=src.at[rows(q),:],dst_ref=ob.at[slot,rows(q),:],send_sem=osend,recv_sem=rsem.at[q],device_id=dst_dev,device_id_type=MESH)
    def arrive(slot,q,rsem):
        pltpu.make_async_copy(ob.at[slot,rows(q),:],ob.at[slot,rows(q),:],rsem.at[q]).wait()
    pl.semaphore_wait(bar,NDEV-1)
    def start_occ(q):
        push(outer,2,q,brecv,o_ref).start()
        push(across,3,q,crecv,o_ref).start()
        push(inner,1,q,arecv,o_ref).start()
    chunks(start_occ)
    def piece(buf,d):
        return buf.at[pl.ds(pl.multiple_of(lax.rem(d,64)*32+(d//64)*16,16),16),:]
    mine=pl.ds(pl.multiple_of(me*16,16),16)
    def t_send(k,c):
        d=lax.rem(me+k,NDEV)
        pltpu.make_async_remote_copy(src_ref=piece(t_ref,d),dst_ref=tc.at[mine,:],send_sem=tsend,recv_sem=trecv,device_id=peer(d),device_id_type=MESH).start()
        return c
    pltpu.make_async_copy(piece(t_ref,me),tc.at[mine,:],trecv).start()
    chunks(lambda q: fwd(0,q))
    mid(0)
    chunks(lambda q: inv([0],q,True))
    def in_a(q):
        arrive(1,q,arecv)
        fwd(1,q)
    chunks(in_a)
    mid(1)
    chunks(lambda q: inv([1],q,False))
    def in_bcd(q):
        arrive(2,q,brecv)
        push(inner,4,q,drecv,ob.at[2]).start()
        fwd(2,q)
        arrive(3,q,crecv)
        fwd(3,q)
        lax.fori_loop(jnp.maximum(32*q,1),32*q+32,t_send,0)
        arrive(4,q,drecv)
        fwd(4,q)
    chunks(in_bcd)
    def mids(j,c):
        mid(j)
        return c
    lax.fori_loop(2,5,mids,0)
    def e_send(k,c):
        d=lax.rem(k,2)*64+k//2
        src=piece(e,d)
        @pl.when(d==me)
        def _(): pltpu.make_async_copy(src,ec.at[mine,:],erecv).start()
        @pl.when(d!=me)
        def _(): pltpu.make_async_remote_copy(src_ref=src,dst_ref=ec.at[mine,:],send_sem=esend,recv_sem=erecv,device_id=peer(d),device_id_type=MESH).start()
        return c
    def tail(q):
        inv([2,3,4],q,False)
        lax.fori_loop(q*4*CP,(q+1)*4*CP,e_send,0)
    chunks(tail)
    whole=lambda buf,n,sem: pltpu.make_async_copy(buf.at[pl.ds(0,n),:],buf.at[pl.ds(0,n),:],sem).wait()
    whole(tc,2048,trecv); whole(tc,2032,tsend)
    whole(ec,2048,erecv); whole(ec,2032,esend)
    for _ in range(4): whole(e,2048,osend)

VM=pl.BlockSpec(memory_space=pltpu.VMEM)
def k1_call(t,o):
    tabs=[jnp.asarray(a) for a in tables()]
    D=pltpu.SemaphoreType.DMA
    big=lambda *n: pltpu.VMEM(n+(2048,128),F32)
    return pl.pallas_call(k1,out_shape=[jax.ShapeDtypeStruct((2048,128),F32)]*2,in_specs=[VM]*6,out_specs=[VM]*2,
      scratch_shapes=[big(5),big(5),big(),big(),D,D((CH,)),D((CH,)),D((CH,)),D((CH,)),D,D,D,D,D],
      compiler_params=pltpu.CompilerParams(collective_id=0,has_side_effects=True,vmem_limit_bytes=40<<20))(t,o,*tabs)

def home(k):
    o=2*(k%32)
    g=(k//32+k%32+(k%32)//4+(k%32)//16)%2
    return g,o
def ar_kernel(n, x_ref, out_ref, parts, sums, ssem, rsem, gsem, hsem):
    g=lax.axis_index("grp"); o=lax.axis_index("orb")
    me=g*64+o
    bar=pltpu.get_barrier_semaphore()
    def sig(k,c):
        d=lax.rem(me+k,128)
        pl.semaphore_signal(bar,inc=1,device_id=(d//64,lax.rem(d,64)),device_id_type=MESH)
        return c
    lax.fori_loop(1,128,sig,0)
    pl.semaphore_wait(bar,127)
    def tile_of(k):
        hg,ho=home(k)
        return hg,ho,(hg==g)&(ho==o)
    def send(k,c):
        hg,ho,mine=tile_of(k)
        src=x_ref.at[pl.ds(pl.multiple_of(k*8,8),8),:]
        @pl.when(mine)
        def _(): pltpu.make_async_copy(src,parts.at[me],rsem).start()
        @pl.when(jnp.logical_not(mine))
        def _(): pltpu.make_async_remote_copy(src_ref=src,dst_ref=parts.at[me],send_sem=ssem,recv_sem=rsem,device_id=(hg,ho),device_id_type=MESH).start()
        return c
    lax.fori_loop(0,n,send,0)
    def work(k,c):
        hg,ho,mine=tile_of(k)
        @pl.when(mine)
        def _():
            pltpu.make_async_copy(parts,parts,rsem).wait()
            sums[...]=jnp.sum(parts[...],axis=0)
            dst=out_ref.at[pl.ds(pl.multiple_of(k*8,8),8),:]
            pltpu.make_async_copy(sums,dst,hsem).start()
            def bc(j,c2):
                d=lax.rem(me+j,128)
                pltpu.make_async_remote_copy(src_ref=sums,dst_ref=dst,send_sem=gsem,recv_sem=hsem,device_id=(d//64,lax.rem(d,64)),device_id_type=MESH).start()
                return c2
            lax.fori_loop(1,128,bc,0)
        return c
    lax.fori_loop(0,n,work,0)
    pltpu.make_async_copy(out_ref,out_ref,hsem).wait()
    def drain(k,c):
        hg,ho,mine=tile_of(k)
        @pl.when(jnp.logical_not(mine))
        def _():
            pltpu.make_async_copy(sums,sums,ssem).wait()
        @pl.when(mine)
        def _():
            pltpu.make_async_copy(parts.at[pl.ds(0,127)],parts.at[pl.ds(0,127)],gsem).wait()
        return c
    lax.fori_loop(0,n,drain,0)
def all_reduce(x, cid=0):
    n=x.shape[0]//8
    vm=pl.BlockSpec(memory_space=pltpu.VMEM)
    return pl.pallas_call(functools.partial(ar_kernel,n),out_shape=jax.ShapeDtypeStruct(x.shape,F32),
      in_specs=[vm],out_specs=vm,
      scratch_shapes=[pltpu.VMEM((128,8,128),F32),pltpu.VMEM((8,128),F32)]+[pltpu.SemaphoreType.DMA]*4,
      compiler_params=pltpu.CompilerParams(collective_id=cid,has_side_effects=True))(x)

STEP_SIZE = 0.3


def swapped(x, axis):
    return lax.ppermute(x, axis, [(0, 1), (1, 0)])


HI = lax.Precision.HIGHEST


def mm(a, b):
    return jnp.dot(a, b, precision=HI)


def mmt(a, b):
    return lax.dot_general(a, b, (((1,), (1,)), ((), ())), precision=HI)


def on_device(occupied, targets, potential):
    g = lax.axis_index("grp")
    T, E = k1_call(targets.reshape(2048, 128), occupied.reshape(2048, 128))
    T = T.reshape(128, 2048)
    E = E.reshape(128, 2048)
    v = lax.dynamic_slice_in_dim(potential, g * 2048, 2048, 0)
    VT = v[None, :] * T
    grams = jnp.concatenate([mmt(E, E), mmt(T, E), mmt(VT, T)], 0) / CELLS
    grams = all_reduce(grams, 1)
    gee, gte, gvt = grams[:128], grams[128:256], grams[256:]
    factor = jnp.linalg.cholesky(gee)
    half = lax.linalg.triangular_solve(factor, gte.T, left_side=True, lower=True)
    mt = lax.linalg.triangular_solve(factor, half, left_side=True, lower=True, transpose_a=True)
    ray = gvt - mm(half.T, half)
    coeff = jnp.concatenate([mt.T, ray], 1)
    both = jnp.concatenate([E, T], 0)

    def rows_of(which):
        c = lax.dynamic_slice_in_dim(coeff, which * 64, 64, 0)
        old = lax.dynamic_slice_in_dim(T, which * 64, 64, 0)
        return old - STEP_SIZE * (v[None, :] * old - mm(c, both))

    theirs = rows_of(1 - g)
    received = swapped(theirs, "grp")
    mine = rows_of(g)
    return jnp.where(g == 0, jnp.concatenate([mine, received], 1), jnp.concatenate([received, mine], 1))


def solution(mesh):
    placed = (P("orb", None), P(("grp", "orb"), None), P("orb"))
    return jax.shard_map(
        on_device, mesh=mesh, in_specs=placed, out_specs=P("grp", "orb"), check_vma=False
    )
```

```python
import functools
import ml_dtypes
import jax
import jax.numpy as jnp
from jax.sharding import PartitionSpec as P
from jax import lax
from jax.experimental import pallas as pl
from jax.experimental.pallas import tpu as pltpu
import numpy as np
BF=jnp.bfloat16; F32=jnp.float32
MESH=pl.DeviceIdType.MESH
CELLS=262144
NDEV=128
CH=4
CP=32//CH
CR=2048//CH

def tables():
    bf=ml_dtypes.bfloat16
    i=np.arange(64)
    ang=2*np.pi*((i[:,None]*i[None,:])%64)/64
    H=(np.cos(ang)+np.sin(ang)).astype(np.float32)
    Hh=H.astype(bf); Hl=(H-Hh.astype(np.float32)).astype(bf)
    perm=2*(i%32)+i//32
    ax=np.concatenate([Hh,Hh,Hl],1)
    ay=ax.reshape(64,3,64)[perm][:,:,perm].reshape(64,192)
    z=np.zeros((64,64),bf)
    bd=lambda m: np.block([[m,z],[z,m]])
    row=np.concatenate([bd(Hh),bd(Hl)],1)
    wz=np.concatenate([row,row],0)
    q=np.minimum(i,64-i).astype(np.float32)*np.float32(2*np.pi/20.0); q2=q*q
    qa=np.broadcast_to((q2+np.float32(0.04))[:,None],(64,128))
    qb=q2.reshape(32,2)
    qr=(qb[:,:,None]+q2[None,None,:]).reshape(32,128)
    return ax,ay,wz,np.concatenate([qa,qr],0).astype(np.float32)

def split(x):
    h=x.astype(BF)
    return h,(x-h.astype(F32)).astype(BF)
def dot(a,b): return jnp.dot(a,b,preferred_element_type=F32)
def half_swap(lo,hi,mask):
    return jnp.where(mask,lo,pltpu.roll(hi,64,1)), jnp.where(mask,pltpu.roll(lo,64,1),hi)
def left(A,planes):
    out=[]
    for k in range(0,len(planes),2):
        h,l=split(jnp.concatenate(planes[k:k+2],1))
        r=dot(A,jnp.concatenate([h,l,h],0))
        out+=[r[:,:128],r[:,128:]]
    return out
def lanes(x,W):
    h,l=split(x)
    r=dot(jnp.concatenate([h,l],1),W)
    return r[:,:128]+r[:,128:]

def peer(d): return (lax.div(d,64),lax.rem(d,64))

def spd_inverse(G):
    n=128
    ri=lax.broadcasted_iota(jnp.int32,(n,n),0); ci=lax.broadcasted_iota(jnp.int32,(n,n),1)
    dg=jnp.where(ri==ci,G,0.0)
    dr=lax.rsqrt(jnp.sum(dg,axis=0,keepdims=True)); dc=lax.rsqrt(jnp.sum(dg,axis=1,keepdims=True))
    sc=dr*dc
    A=G*sc
    lane=lax.broadcasted_iota(jnp.int32,(1,n),1); sub=lax.broadcasted_iota(jnp.int32,(n,1),0)
    for k in range(n):
        r=A[k:k+1,:]; c=A[:,k:k+1]; d=A[k:k+1,k:k+1]
        v=(r+(lane==k).astype(F32))*(1.0/d)
        u=c-(sub==k).astype(F32)
        A=A-u*v
    return A*sc


def home(k):
    o=2*lax.rem(k,32)
    g=lax.rem(lax.div(k,32)+lax.rem(k,32)+lax.div(lax.rem(k,32),4)+lax.div(lax.rem(k,32),16),2)
    return g*64+o

def mega(t_hbm,o_hbm,p_hbm,ax_hbm,ay_hbm,wz_hbm,q_hbm,out,tc,ec,t_ref,vp,ax_ref,ay_ref,wz_ref,q_ref,xh,xl,part,gs,parts,sums,ub,ob,sb,kt,e,osend,arecv,brecv,crecv,drecv,tsend,trecv,esend,erecv,loc,tabs,rsend,rrecv,gsend,grecv,usend,urecv):
    g=lax.axis_index("grp"); o=lax.axis_index("orb"); me=g*64+o
    s=2*lax.rem(o,2)-1
    w=lambda v: lax.rem(v+128,64)
    inner=(g,w(o-s)); outer=(g,w(o+s)); across=(g,w(o-2*s))
    copies=[pltpu.make_async_copy(a,b,tabs.at[i]) for i,(a,b) in enumerate(((q_hbm,q_ref),(o_hbm,ob.at[0]),(t_hbm,t_ref),(ax_hbm,ax_ref),(ay_hbm,ay_ref),(wz_hbm,wz_ref),(p_hbm,vp)))]
    for c in copies: c.start()
    bar=pltpu.get_barrier_semaphore()
    def sig(k,c):
        pl.semaphore_signal(bar,inc=1,device_id=peer(lax.rem(me+k,NDEV)),device_id_type=MESH)
        return c
    lax.fori_loop(1,NDEV,sig,0)
    mask=lax.broadcasted_iota(jnp.int32,(32,128),1)<64
    copies[0].wait()
    qa=q_ref[0:64,:]
    def ktab(r,c):
        kt[pl.ds(pl.multiple_of(r*64,64),64),:]=(4*np.pi/CELLS)/(qa+q_ref[pl.ds(64+r,1),:])
        return c
    lax.fori_loop(0,32,ktab,0,unroll=8)
    for c in copies[1:]: c.wait()
    ax=ax_ref[...];ay=ay_ref[...];wz=wz_ref[...]
    o_ref=ob.at[0]
    def rows(q): return pl.ds(pl.multiple_of(q*CR,CR),CR)
    def fwd(j,q):
        pr=t_ref[rows(q),:]*ob[j,rows(q),:]
        b=[]
        for p in range(CP):
            b+=half_swap(pr[64*p:64*p+32],pr[64*p+32:64*p+64],mask)
        x=lanes(jnp.concatenate(b,0),wz)
        f=left(ay,[x[64*p:64*p+64] for p in range(CP)])
        out=[]
        for p in range(CP): out+=half_swap(f[p][:32],f[p][32:],mask)
        sb[j,rows(q),:]=jnp.concatenate(out,0)
    R=16
    def mid(j):
        def half(i,c):
            f=left(ax,[sb[j,pl.ds(i*R+r,64,stride=32),:] for r in range(R)])
            kk=kt[pl.ds(pl.multiple_of(i*R*64,R*64),R*64),:]
            f=left(ax,[f[r]*kk[64*r:64*r+64] for r in range(R)])
            for r in range(R): sb[j,pl.ds(i*R+r,64,stride=32),:]=f[r]
            return c
        lax.fori_loop(0,32//R,half,0)
    def inv(js,q,first):
        b=[]
        for j in js:
            sv=sb[j,rows(q),:]
            for p in range(CP):
                u,v=half_swap(sv[64*p:64*p+32],sv[64*p+32:64*p+64],mask)
                b.append(jnp.concatenate([u,v],0))
        x=lanes(jnp.concatenate(left(ay,b),0),wz)
        acc=None if first else e[rows(q),:]
        for n,j in enumerate(js):
            out=[]
            for p in range(CP):
                k=64*(n*CP+p)
                out+=half_swap(x[k:k+32],x[k+32:k+64],mask)
            term=jnp.concatenate(out,0)*ob[j,rows(q),:]
            acc=-term if acc is None else acc-term
        e[rows(q),:]=acc
    def chunks(f):
        def body(q,c):
            f(q)
            return c
        lax.fori_loop(0,CH,body,0)
    def push(dst_dev,slot,q,rsem,src):
        return pltpu.make_async_remote_copy(src_ref=src.at[rows(q),:],dst_ref=ob.at[slot,rows(q),:],send_sem=osend,recv_sem=rsem.at[q],device_id=dst_dev,device_id_type=MESH)
    def arrive(slot,q,rsem):
        pltpu.make_async_copy(ob.at[slot,rows(q),:],ob.at[slot,rows(q),:],rsem.at[q]).wait()
    pl.semaphore_wait(bar,NDEV-1)
    def start_occ(q):
        push(outer,2,q,brecv,o_ref).start()
        push(across,3,q,crecv,o_ref).start()
        push(inner,1,q,arecv,o_ref).start()
    chunks(start_occ)
    def piece(buf,d):
        return buf.at[pl.ds(pl.multiple_of(lax.rem(d,64)*32+lax.div(d,64)*16,16),16),:]
    mine=pl.ds(pl.multiple_of(me*16,16),16)
    def t_send(k,c):
        d=lax.rem(me+k,NDEV)
        pltpu.make_async_remote_copy(src_ref=piece(t_ref,d),dst_ref=tc.at[mine,:],send_sem=tsend,recv_sem=trecv,device_id=peer(d),device_id_type=MESH).start()
        return c
    pltpu.make_async_copy(piece(t_ref,me),tc.at[mine,:],trecv).start()
    chunks(lambda q: fwd(0,q))
    mid(0)
    chunks(lambda q: inv([0],q,True))
    def in_a(q):
        arrive(1,q,arecv)
        fwd(1,q)
    chunks(in_a)
    mid(1)
    chunks(lambda q: inv([1],q,False))
    def in_bcd(q):
        arrive(2,q,brecv)
        push(inner,4,q,drecv,ob.at[2]).start()
        fwd(2,q)
        arrive(3,q,crecv)
        fwd(3,q)
        lax.fori_loop(jnp.maximum(32*q,1),32*q+32,t_send,0)
        arrive(4,q,drecv)
        fwd(4,q)
    chunks(in_bcd)
    def mids(j,c):
        mid(j)
        return c
    lax.fori_loop(2,5,mids,0)
    def e_send(k,c):
        d=lax.rem(k,2)*64+lax.div(k,2)
        src=piece(e,d)
        @pl.when(d==me)
        def _(): pltpu.make_async_copy(src,ec.at[mine,:],erecv).start()
        @pl.when(d!=me)
        def _(): pltpu.make_async_remote_copy(src_ref=src,dst_ref=ec.at[mine,:],send_sem=esend,recv_sem=erecv,device_id=peer(d),device_id_type=MESH).start()
        return c
    def tail(q):
        inv([2,3,4],q,False)
        lax.fori_loop(q*4*CP,(q+1)*4*CP,e_send,0)
    chunks(tail)
    whole=lambda buf,n,sem: pltpu.make_async_copy(buf.at[pl.ds(0,n),:],buf.at[pl.ds(0,n),:],sem).wait()
    def spread(lo,hi):
        def send(n,c):
            src=part.at[pl.ds(pl.multiple_of(n*8,8),8),:]
            h=home(n)
            @pl.when(h==me)
            def _(): pltpu.make_async_copy(src,parts.at[me],rrecv).start()
            @pl.when(h!=me)
            def _(): pltpu.make_async_remote_copy(src_ref=src,dst_ref=parts.at[me],send_sem=rsend,recv_sem=rrecv,device_id=peer(h),device_id_type=MESH).start()
            return c
        lax.fori_loop(lo,hi,send,0)
    def nt(a,b): return lax.dot_general(a,b,(((1,),(1,)),((),())),preferred_element_type=F32)
    def rowset(buf,s): return buf[pl.ds(s,128,stride=16),:]
    def vrow(s): return vp[pl.ds(g*16+s,1),:]
    whole(tc,2048,trecv)
    for s in range(16):
        h,l=split(rowset(tc,s))
        xh[128:256,128*s:128*s+128]=h; xl[128:256,128*s:128*s+128]=l
        h,l=split(rowset(tc,s)*vrow(s))
        xh[0:128,128*s:128*s+128]=h; xl[0:128,128*s:128*s+128]=l
    part[256:384,:]=(nt(xh[0:128,:],xh[128:256,:])+nt(xh[0:128,:],xl[128:256,:])+nt(xl[0:128,:],xh[128:256,:]))*(1.0/CELLS)
    spread(32,48)
    whole(ec,2048,erecv)
    for s in range(16):
        h,l=split(rowset(ec,s))
        xh[0:128,128*s:128*s+128]=h; xl[0:128,128*s:128*s+128]=l
    part[0:256,:]=(nt(xh[...],xh[0:128,:])+nt(xh[...],xl[0:128,:])+nt(xl[...],xh[0:128,:]))*(1.0/CELLS)
    spread(0,32)
    def gather(n,c):
        @pl.when(home(n)==me)
        def _():
            pltpu.make_async_copy(parts,parts,rrecv).wait()
            sums[...]=jnp.sum(parts[...],axis=0)
            dst=gs.at[pl.ds(pl.multiple_of(n*8,8),8),:]
            pltpu.make_async_copy(sums,dst,grecv).start()
            def bc(j,c2):
                pltpu.make_async_remote_copy(src_ref=sums,dst_ref=dst,send_sem=gsend,recv_sem=grecv,device_id=peer(lax.rem(me+j,NDEV)),device_id_type=MESH).start()
                return c2
            lax.fori_loop(1,NDEV,bc,0)
        return c
    lax.fori_loop(0,48,gather,0)
    pltpu.make_async_copy(gs,gs,grecv).wait()
    HI=lax.Precision.HIGHEST
    gte=gs[128:256,:]
    m=jnp.dot(gte,spd_inverse(gs[0:128,:]),precision=HI,preferred_element_type=F32)
    ray=gs[256:384,:]-lax.dot_general(m,gte,(((1,),(1,)),((),())),precision=HI,preferred_element_type=F32)
    ch,cl=split(jnp.concatenate([m,ray],1))
    sb[0,0:128,:]=m; sb[0,128:256,:]=ray
    def coeff(which):
        b=which*64
        h0,l0=split(sb[0,pl.ds(pl.multiple_of(b,64),64),:]); h1,l1=split(sb[0,pl.ds(pl.multiple_of(128+b,64),64),:])
        return jnp.concatenate([h0,h1],1),jnp.concatenate([l0,l1],1)
    def rows_of(which,s,n):
        h,l=coeff(which)
        c=slice(128*s,128*(s+n))
        r=dot(h,xh[:,c])+dot(h,xl[:,c])+dot(l,xh[:,c])
        old=jnp.concatenate([tc[pl.ds(which*1024+s+i,64,stride=16),:] for i in range(n)],1)
        v=jnp.concatenate([vrow(s+i) for i in range(n)],1)
        return old-0.3*(v*old-r)
    other=1-g
    cols=lambda s,n: pl.ds(pl.multiple_of(g*2048+128*s,128),128*n)
    N=4
    def swap_copy(s): return pltpu.make_async_remote_copy(src_ref=ub.at[:,pl.ds(128*s,128*N)],dst_ref=out.at[:,cols(s,N)],send_sem=usend.at[s//N],recv_sem=urecv.at[s//N],device_id=(other,o),device_id_type=MESH)
    for s in range(0,16,N):
        ub[:,128*s:128*(s+N)]=rows_of(other,s,N)
        swap_copy(s).start()
    for s in range(0,16,N):
        out[:,cols(s,N)]=rows_of(g,s,N)
    for s in range(0,16,N): swap_copy(s).wait()
    def drain(n,c):
        @pl.when(home(n)!=me)
        def _(): pltpu.make_async_copy(sums,sums,rsend).wait()
        @pl.when(home(n)==me)
        def _(): pltpu.make_async_copy(parts.at[pl.ds(0,127)],parts.at[pl.ds(0,127)],gsend).wait()
        return c
    lax.fori_loop(0,48,drain,0)
    whole(tc,2032,tsend); whole(ec,2032,esend)
    for _ in range(4): whole(e,2048,osend)

VM=pl.BlockSpec(memory_space=pltpu.VMEM)
ANY=pl.BlockSpec(memory_space=pl.ANY)
def mega_call(t,o,p):
    tabs=[jnp.asarray(a) for a in tables()]
    D=pltpu.SemaphoreType.DMA
    big=lambda *n: pltpu.VMEM(n+(2048,128),F32)
    return pl.pallas_call(mega,out_shape=jax.ShapeDtypeStruct((64,4096),F32),in_specs=[ANY]*7,out_specs=VM,
      scratch_shapes=[big(),big(),big(),pltpu.VMEM((32,128),F32),pltpu.VMEM((64,192),BF),pltpu.VMEM((64,192),BF),pltpu.VMEM((256,256),BF),pltpu.VMEM((96,128),F32),
        pltpu.VMEM((256,2048),BF),pltpu.VMEM((256,2048),BF),pltpu.VMEM((384,128),F32),pltpu.VMEM((384,128),F32),pltpu.VMEM((128,8,128),F32),pltpu.VMEM((8,128),F32),pltpu.VMEM((64,2048),F32),
        big(5),big(5),big(),big(),D,D((CH,)),D((CH,)),D((CH,)),D((CH,)),D,D,D,D,D,D((7,)),D,D,D,D,D((4,)),D((4,))],
      compiler_params=pltpu.CompilerParams(collective_id=0,has_side_effects=True,vmem_limit_bytes=58<<20))(t,o,p,*tabs)

def on_device(occupied, targets, potential):
    return mega_call(targets.reshape(2048, 128), occupied.reshape(2048, 128), potential.reshape(32, 128))


def solution(mesh):
    placed = (P("orb", None), P(("grp", "orb"), None), P("orb"))
    return jax.shard_map(
        on_device, mesh=mesh, in_specs=placed, out_specs=P("grp", "orb"), check_vma=False
    )
```

```python
import functools
import ml_dtypes
import jax
import jax.numpy as jnp
from jax.sharding import PartitionSpec as P
from jax import lax
from jax.experimental import pallas as pl
from jax.experimental.pallas import tpu as pltpu
import numpy as np
BF=jnp.bfloat16; F32=jnp.float32
MESH=pl.DeviceIdType.MESH
CELLS=262144
NDEV=128
CH=4
CP=32//CH
CR=2048//CH

def tables():
    bf=ml_dtypes.bfloat16
    i=np.arange(64)
    ang=2*np.pi*((i[:,None]*i[None,:])%64)/64
    H=(np.cos(ang)+np.sin(ang)).astype(np.float32)
    Hh=H.astype(bf); Hl=(H-Hh.astype(np.float32)).astype(bf)
    perm=2*(i%32)+i//32
    ax=np.concatenate([Hh,Hh,Hl],1)
    ay=ax.reshape(64,3,64)[perm][:,:,perm].reshape(64,192)
    z=np.zeros((64,64),bf)
    bd=lambda m: np.block([[m,z],[z,m]])
    row=np.concatenate([bd(Hh),bd(Hl)],1)
    wz=np.concatenate([row,row],0)
    q=np.minimum(i,64-i).astype(np.float32)*np.float32(2*np.pi/20.0); q2=q*q
    qa=np.broadcast_to((q2+np.float32(0.04))[:,None],(64,128))
    qb=q2.reshape(32,2)
    qr=(qb[:,:,None]+q2[None,None,:]).reshape(32,128)
    return ax,ay,wz,np.concatenate([qa,qr],0).astype(np.float32)

def split(x):
    h=x.astype(BF)
    return h,(x-h.astype(F32)).astype(BF)
def dot(a,b): return jnp.dot(a,b,preferred_element_type=F32)
def half_swap(lo,hi,mask):
    return jnp.where(mask,lo,pltpu.roll(hi,64,1)), jnp.where(mask,pltpu.roll(lo,64,1),hi)
def left(A,planes):
    out=[]
    for k in range(0,len(planes),2):
        h,l=split(jnp.concatenate(planes[k:k+2],1))
        r=dot(A,jnp.concatenate([h,l,h],0))
        out+=[r[:,:128],r[:,128:]]
    return out
def lanes(x,W):
    h,l=split(x)
    r=dot(jnp.concatenate([h,l],1),W)
    return r[:,:128]+r[:,128:]

def peer(d): return (lax.div(d,64),lax.rem(d,64))

NB=8
def recip(x):
    y=pl.reciprocal(x,approx=True)
    y=y*(2.0-x*y)
    return y*(2.0-x*y)
def block_cols(Bp,k,sub):
    a={}
    for i in range(NB):
        for j in range(i,NB):
            a[i,j]=jnp.broadcast_to(Bp[i:i+1,k+j:k+j+1],(NB,128))
    g=lambda i,j: a[min(i,j),max(i,j)]
    for q in range(NB):
        rd=recip(a[q,q])
        c=[g(i,q) for i in range(NB)]
        t=[c[i]*rd for i in range(NB)]
        for i in range(NB):
            for j in range(i,NB):
                if i!=q and j!=q: a[i,j]=a[i,j]-c[i]*t[j]
        for i in range(NB):
            if i!=q: a[min(i,q),max(i,q)]=t[i]
        a[q,q]=-rd
    cols=[]
    for j in range(NB):
        v=g(0,j)
        for i in range(1,NB): v=jnp.where(sub==i,g(i,j),v)
        cols.append(-v)
    return cols
def tree(xs):
    while len(xs)>1: xs=[xs[i]+xs[i+1] if i+1<len(xs) else xs[i] for i in range(0,len(xs),2)]
    return xs[0]

def spd_inverse(G):
    n=128
    ri=lax.broadcasted_iota(jnp.int32,(n,n),0); ci=lax.broadcasted_iota(jnp.int32,(n,n),1)
    dg=jnp.where(ri==ci,G,0.0)
    sc=lax.rsqrt(jnp.sum(dg,axis=0,keepdims=True))*lax.rsqrt(jnp.sum(dg,axis=1,keepdims=True))
    A=G*sc
    lane=lax.broadcasted_iota(jnp.int32,(8,n),1); sub=lax.broadcasted_iota(jnp.int32,(8,n),0)
    rows=[A[8*i:8*i+8,:] for i in range(16)]
    nxt=rows[0]
    for p in range(16):
        k=8*p
        eye=(lane==sub+k).astype(F32)
        cols=block_cols(nxt,k,sub)
        R=nxt+eye
        W=tree([cols[j]*R[j:j+1,:] for j in range(NB)])
        wj=[W[j:j+1,:] for j in range(NB)]
        upd=lambda a: a-tree([a[:,k+j:k+j+1]*wj[j] for j in range(NB)])
        if p<15: nxt=upd(rows[p+1])
        rows=[W-eye if i==p else nxt if i==p+1 else upd(rows[i]) for i in range(16)]
    return jnp.concatenate(rows,0)*sc


def home(k):
    o=2*lax.rem(k,32)
    g=lax.rem(lax.div(k,32)+lax.rem(k,32)+lax.div(lax.rem(k,32),4)+lax.div(lax.rem(k,32),16),2)
    return g*64+o

def mega(t_hbm,o_hbm,p_hbm,ax_hbm,ay_hbm,wz_hbm,q_hbm,out,tc,ec,t_ref,vp,ax_ref,ay_ref,wz_ref,q_ref,xh,xl,part,gs,parts,sums,ub,ob,sb,kt,e,osend,arecv,brecv,crecv,drecv,tsend,trecv,esend,erecv,loc,tabs,rsend,rrecv,gsend,grecv,usend,urecv):
    g=lax.axis_index("grp"); o=lax.axis_index("orb"); me=g*64+o
    s=2*lax.rem(o,2)-1
    w=lambda v: lax.rem(v+128,64)
    inner=(g,w(o-s)); outer=(g,w(o+s)); across=(g,w(o-2*s))
    copies=[pltpu.make_async_copy(a,b,tabs.at[i]) for i,(a,b) in enumerate(((q_hbm,q_ref),(o_hbm,ob.at[0]),(t_hbm,t_ref),(ax_hbm,ax_ref),(ay_hbm,ay_ref),(wz_hbm,wz_ref),(p_hbm,vp)))]
    for c in copies: c.start()
    bar=pltpu.get_barrier_semaphore()
    def sig(k,c):
        pl.semaphore_signal(bar,inc=1,device_id=peer(lax.rem(me+k,NDEV)),device_id_type=MESH)
        return c
    lax.fori_loop(1,NDEV,sig,0)
    mask=lax.broadcasted_iota(jnp.int32,(32,128),1)<64
    copies[0].wait()
    qa=q_ref[0:64,:]
    def ktab(r,c):
        kt[pl.ds(pl.multiple_of(r*64,64),64),:]=(4*np.pi/CELLS)/(qa+q_ref[pl.ds(64+r,1),:])
        return c
    lax.fori_loop(0,32,ktab,0,unroll=8)
    for c in copies[1:]: c.wait()
    ax=ax_ref[...];ay=ay_ref[...];wz=wz_ref[...]
    o_ref=ob.at[0]
    def rows(q): return pl.ds(pl.multiple_of(q*CR,CR),CR)
    def fwd(j,q):
        pr=t_ref[rows(q),:]*ob[j,rows(q),:]
        b=[]
        for p in range(CP):
            b+=half_swap(pr[64*p:64*p+32],pr[64*p+32:64*p+64],mask)
        x=lanes(jnp.concatenate(b,0),wz)
        f=left(ay,[x[64*p:64*p+64] for p in range(CP)])
        out=[]
        for p in range(CP): out+=half_swap(f[p][:32],f[p][32:],mask)
        sb[j,rows(q),:]=jnp.concatenate(out,0)
    R=16
    def mid(j):
        def half(i,c):
            f=left(ax,[sb[j,pl.ds(i*R+r,64,stride=32),:] for r in range(R)])
            kk=kt[pl.ds(pl.multiple_of(i*R*64,R*64),R*64),:]
            f=left(ax,[f[r]*kk[64*r:64*r+64] for r in range(R)])
            for r in range(R): sb[j,pl.ds(i*R+r,64,stride=32),:]=f[r]
            return c
        lax.fori_loop(0,32//R,half,0)
    def inv(js,q,first):
        b=[]
        for j in js:
            sv=sb[j,rows(q),:]
            for p in range(CP):
                u,v=half_swap(sv[64*p:64*p+32],sv[64*p+32:64*p+64],mask)
                b.append(jnp.concatenate([u,v],0))
        x=lanes(jnp.concatenate(left(ay,b),0),wz)
        acc=None if first else e[rows(q),:]
        for n,j in enumerate(js):
            out=[]
            for p in range(CP):
                k=64*(n*CP+p)
                out+=half_swap(x[k:k+32],x[k+32:k+64],mask)
            term=jnp.concatenate(out,0)*ob[j,rows(q),:]
            acc=-term if acc is None else acc-term
        e[rows(q),:]=acc
    def chunks(f):
        def body(q,c):
            f(q)
            return c
        lax.fori_loop(0,CH,body,0)
    def push(dst_dev,slot,q,rsem,src):
        return pltpu.make_async_remote_copy(src_ref=src.at[rows(q),:],dst_ref=ob.at[slot,rows(q),:],send_sem=osend,recv_sem=rsem.at[q],device_id=dst_dev,device_id_type=MESH)
    def arrive(slot,q,rsem):
        pltpu.make_async_copy(ob.at[slot,rows(q),:],ob.at[slot,rows(q),:],rsem.at[q]).wait()
    chunks(lambda q: fwd(0,q))
    pl.semaphore_wait(bar,NDEV-1)
    def alone(v):
        c=lax.rem(lax.div(v,2),16)
        return ((c==3)|(c==12)).astype(jnp.int32)
    single=alone(o)
    def order(i,a=single):
        f=3*g*(1-a)
        return i+jnp.where(i==0,f,jnp.where(i==3,-f,0))
    f3=order(0)
    on_out,on_across=alone(w(o+s)),alone(w(o-2*s))
    twin=(1-g,o)
    def start_a(q): push(inner,1,q,arecv,o_ref).start()
    def loop(lo,hi,f):
        def body(i,c):
            f(i)
            return c
        lax.fori_loop(lo,hi,body,0)
    def start_bc(i):
        @pl.when(i<3+on_out)
        def _(): push(outer,2,order(i,on_out),brecv,o_ref).start()
        @pl.when(i<3+on_across)
        def _(): push(across,3,order(i,on_across),crecv,o_ref).start()
    loop(0,4,start_bc)
    chunks(start_a)
    def piece(buf,d):
        return buf.at[pl.ds(pl.multiple_of(lax.rem(d,64)*32+lax.div(d,64)*16,16),16),:]
    mine=pl.ds(pl.multiple_of(me*16,16),16)
    def t_send(k):
        d=lax.rem(me+45*k,NDEV)
        pltpu.make_async_remote_copy(src_ref=piece(t_ref,d),dst_ref=tc.at[mine,:],send_sem=tsend,recv_sem=trecv,device_id=peer(d),device_id_type=MESH).start()
    pltpu.make_async_copy(piece(t_ref,me),tc.at[mine,:],trecv).start()
    mid(0)
    chunks(lambda q: inv([0],q,True))
    def in_a(q):
        arrive(1,q,arecv)
        fwd(1,q)
    chunks(in_a)
    mid(1)
    arrive(2,f3,brecv)
    @pl.when(single==0)
    def _(): push(twin,2,f3,brecv,ob.at[2]).start()
    push(inner,4,f3,drecv,ob.at[2]).start()
    arrive(3,f3,crecv)
    @pl.when(single==0)
    def _(): push(twin,3,f3,crecv,ob.at[3]).start()
    chunks(lambda q: inv([1],q,False))
    def in_bcd(i):
        q=order(i)
        @pl.when(i>0)
        def _():
            arrive(2,q,brecv)
            push(inner,4,q,drecv,ob.at[2]).start()
        fwd(2,q)
        @pl.when(i>0)
        def _(): arrive(3,q,crecv)
        fwd(3,q)
        arrive(4,q,drecv)
        fwd(4,q)
    loop(0,3,in_bcd)
    loop(3,4,in_bcd)
    loop(1,NDEV,t_send)
    mid(2)
    mid(3)
    mid(4)
    def e_send(k,c):
        d=lax.rem(k,2)*64+lax.div(k,2)
        src=piece(e,d)
        @pl.when(d==me)
        def _(): pltpu.make_async_copy(src,ec.at[mine,:],erecv).start()
        @pl.when(d!=me)
        def _(): pltpu.make_async_remote_copy(src_ref=src,dst_ref=ec.at[mine,:],send_sem=esend,recv_sem=erecv,device_id=peer(d),device_id_type=MESH).start()
        return c
    def tail(q):
        inv([2,3,4],q,False)
        lax.fori_loop(q*4*CP,(q+1)*4*CP,e_send,0)
    chunks(tail)
    whole=lambda buf,n,sem: pltpu.make_async_copy(buf.at[pl.ds(0,n),:],buf.at[pl.ds(0,n),:],sem).wait()
    def spread(lo,hi):
        def send(n,c):
            src=part.at[pl.ds(pl.multiple_of(n*8,8),8),:]
            h=home(n)
            @pl.when(h==me)
            def _(): pltpu.make_async_copy(src,parts.at[me],rrecv).start()
            @pl.when(h!=me)
            def _(): pltpu.make_async_remote_copy(src_ref=src,dst_ref=parts.at[me],send_sem=rsend,recv_sem=rrecv,device_id=peer(h),device_id_type=MESH).start()
            return c
        lax.fori_loop(lo,hi,send,0)
    def nt(a,b): return lax.dot_general(a,b,(((1,),(1,)),((),())),preferred_element_type=F32)
    def rowset(buf,s): return buf[pl.ds(s,128,stride=16),:]
    def vrow(s): return vp[pl.ds(g*16+s,1),:]
    whole(tc,2048,trecv)
    for s in range(16):
        h,l=split(rowset(tc,s))
        xh[128:256,128*s:128*s+128]=h; xl[128:256,128*s:128*s+128]=l
        h,l=split(rowset(tc,s)*vrow(s))
        xh[0:128,128*s:128*s+128]=h; xl[0:128,128*s:128*s+128]=l
    part[256:384,:]=(nt(xh[0:128,:],xh[128:256,:])+nt(xh[0:128,:],xl[128:256,:])+nt(xl[0:128,:],xh[128:256,:]))*(1.0/CELLS)
    spread(32,48)
    whole(ec,2048,erecv)
    for s in range(16):
        h,l=split(rowset(ec,s))
        xh[0:128,128*s:128*s+128]=h; xl[0:128,128*s:128*s+128]=l
    part[0:256,:]=(nt(xh[...],xh[0:128,:])+nt(xh[...],xl[0:128,:])+nt(xl[...],xh[0:128,:]))*(1.0/CELLS)
    spread(0,32)
    def gather(n,c):
        @pl.when(home(n)==me)
        def _():
            pltpu.make_async_copy(parts,parts,rrecv).wait()
            sums[...]=jnp.sum(parts[...],axis=0)
            dst=gs.at[pl.ds(pl.multiple_of(n*8,8),8),:]
            pltpu.make_async_copy(sums,dst,grecv).start()
            def bc(j,c2):
                step=lambda v: jnp.where(v<2,2+v,3-v)
                dz,dy,dx=step(lax.div(j,32)),step(lax.rem(lax.div(j,8),4)),step(lax.rem(lax.div(j,2),4))
                y=lax.rem(2*lax.div(o,32)+g+dy,4)
                z=lax.rem(lax.div(o,8)+dz,4)
                x=lax.rem(lax.div(o,2)+dx,4)
                c=lax.rem(o+1+j,2)
                pltpu.make_async_remote_copy(src_ref=sums,dst_ref=dst,send_sem=gsend,recv_sem=grecv,device_id=(lax.rem(y,2),lax.div(y,2)*32+z*8+x*2+c),device_id_type=MESH).start()
                return c2
            lax.fori_loop(0,NDEV-1,bc,0)
        return c
    lax.fori_loop(0,48,gather,0)
    pltpu.make_async_copy(gs,gs,grecv).wait()
    HI=lax.Precision.HIGHEST
    gte=gs[128:256,:]
    m=jnp.dot(gte,spd_inverse(gs[0:128,:]),precision=HI,preferred_element_type=F32)
    ray=gs[256:384,:]-lax.dot_general(m,gte,(((1,),(1,)),((),())),precision=HI,preferred_element_type=F32)
    ch,cl=split(jnp.concatenate([m,ray],1))
    sb[0,0:128,:]=m; sb[0,128:256,:]=ray
    def coeff(which):
        b=which*64
        h0,l0=split(sb[0,pl.ds(pl.multiple_of(b,64),64),:]); h1,l1=split(sb[0,pl.ds(pl.multiple_of(128+b,64),64),:])
        return jnp.concatenate([h0,h1],1),jnp.concatenate([l0,l1],1)
    def rows_of(which,s,n):
        h,l=coeff(which)
        c=slice(128*s,128*(s+n))
        r=dot(h,xh[:,c])+dot(h,xl[:,c])+dot(l,xh[:,c])
        old=jnp.concatenate([tc[pl.ds(which*1024+s+i,64,stride=16),:] for i in range(n)],1)
        v=jnp.concatenate([vrow(s+i) for i in range(n)],1)
        return old-0.3*(v*old-r)
    other=1-g
    cols=lambda s,n: pl.ds(pl.multiple_of(g*2048+128*s,128),128*n)
    N=4
    def swap_copy(s): return pltpu.make_async_remote_copy(src_ref=ub.at[:,pl.ds(128*s,128*N)],dst_ref=out.at[:,cols(s,N)],send_sem=usend.at[s//N],recv_sem=urecv.at[s//N],device_id=(other,o),device_id_type=MESH)
    for s in range(0,16,N):
        ub[:,128*s:128*(s+N)]=rows_of(other,s,N)
        swap_copy(s).start()
    for s in range(0,16,N):
        out[:,cols(s,N)]=rows_of(g,s,N)
    def drain(n,c):
        @pl.when(home(n)!=me)
        def _(): pltpu.make_async_copy(sums,sums,rsend).wait()
        @pl.when(home(n)==me)
        def _(): pltpu.make_async_copy(parts.at[pl.ds(0,127)],parts.at[pl.ds(0,127)],gsend).wait()
        return c
    lax.fori_loop(0,48,drain,0)
    whole(tc,2032,tsend); whole(ec,2032,esend)
    def drain_occ(i,c):
        pltpu.make_async_copy(ob.at[0,rows(0),:],ob.at[0,rows(0),:],osend).wait()
        return c
    lax.fori_loop(0,16+on_out+on_across-2*single,drain_occ,0)
    for s in range(0,16,N): swap_copy(s).wait()

VM=pl.BlockSpec(memory_space=pltpu.VMEM)
ANY=pl.BlockSpec(memory_space=pl.ANY)
def mega_call(t,o,p):
    tabs=[jnp.asarray(a) for a in tables()]
    D=pltpu.SemaphoreType.DMA
    big=lambda *n: pltpu.VMEM(n+(2048,128),F32)
    return pl.pallas_call(mega,out_shape=jax.ShapeDtypeStruct((64,4096),F32),in_specs=[ANY]*7,out_specs=VM,
      scratch_shapes=[big(),big(),big(),pltpu.VMEM((32,128),F32),pltpu.VMEM((64,192),BF),pltpu.VMEM((64,192),BF),pltpu.VMEM((256,256),BF),pltpu.VMEM((96,128),F32),
        pltpu.VMEM((256,2048),BF),pltpu.VMEM((256,2048),BF),pltpu.VMEM((384,128),F32),pltpu.VMEM((384,128),F32),pltpu.VMEM((128,8,128),F32),pltpu.VMEM((8,128),F32),pltpu.VMEM((64,2048),F32),
        big(5),big(5),big(),big(),D,D((CH,)),D((CH,)),D((CH,)),D((CH,)),D,D,D,D,D,D((7,)),D,D,D,D,D((4,)),D((4,))],
      compiler_params=pltpu.CompilerParams(collective_id=0,has_side_effects=True,vmem_limit_bytes=58<<20))(t,o,p,*tabs)

def on_device(occupied, targets, potential):
    return mega_call(targets.reshape(2048, 128), occupied.reshape(2048, 128), potential.reshape(32, 128))


def solution(mesh):
    placed = (P("orb", None), P(("grp", "orb"), None), P("orb"))
    return jax.shard_map(
        on_device, mesh=mesh, in_specs=placed, out_specs=P("grp", "orb"), check_vma=False
    )
```

```python
import functools
import ml_dtypes
import jax
import jax.numpy as jnp
from jax.sharding import PartitionSpec as P
from jax import lax
from jax.experimental import pallas as pl
from jax.experimental.pallas import tpu as pltpu
import numpy as np
BF=jnp.bfloat16; F32=jnp.float32
MESH=pl.DeviceIdType.MESH
CELLS=262144
NDEV=128
CH=4
CP=32//CH
CR=2048//CH

def tables():
    bf=ml_dtypes.bfloat16
    i=np.arange(64)
    ang=2*np.pi*((i[:,None]*i[None,:])%64)/64
    H=(np.cos(ang)+np.sin(ang)).astype(np.float32)
    Hh=H.astype(bf); Hl=(H-Hh.astype(np.float32)).astype(bf)
    perm=2*(i%32)+i//32
    ax=np.concatenate([Hh,Hh,Hl],1)
    ay=ax.reshape(64,3,64)[perm][:,:,perm].reshape(64,192)
    z=np.zeros((64,64),bf)
    bd=lambda m: np.block([[m,z],[z,m]])
    row=np.concatenate([bd(Hh),bd(Hl)],1)
    wz=np.concatenate([row,row],0)
    q=np.minimum(i,64-i).astype(np.float32)*np.float32(2*np.pi/20.0); q2=q*q
    qa=np.broadcast_to((q2+np.float32(0.04))[:,None],(64,128))
    qb=q2.reshape(32,2)
    qr=(qb[:,:,None]+q2[None,None,:]).reshape(32,128)
    return ax,ay,wz,np.concatenate([qa,qr],0).astype(np.float32)

def split(x):
    h=x.astype(BF)
    return h,(x-h.astype(F32)).astype(BF)
def dot(a,b): return jnp.dot(a,b,preferred_element_type=F32)
def half_swap(lo,hi,mask):
    return jnp.where(mask,lo,pltpu.roll(hi,64,1)), jnp.where(mask,pltpu.roll(lo,64,1),hi)
def left(A,planes):
    out=[]
    for k in range(0,len(planes),2):
        h,l=split(jnp.concatenate(planes[k:k+2],1))
        r=dot(A,jnp.concatenate([h,l,h],0))
        out+=[r[:,:128],r[:,128:]]
    return out
def lanes(x,W):
    h,l=split(x)
    r=dot(jnp.concatenate([h,l],1),W)
    return r[:,:128]+r[:,128:]

def peer(d): return (lax.div(d,64),lax.rem(d,64))

NB=8
def recip(x):
    y=pl.reciprocal(x,approx=True)
    y=y*(2.0-x*y)
    return y*(2.0-x*y)
def block_cols(Bp,k,sub):
    a={}
    for i in range(NB):
        for j in range(i,NB):
            a[i,j]=jnp.broadcast_to(Bp[i:i+1,k+j:k+j+1],(NB,128))
    g=lambda i,j: a[min(i,j),max(i,j)]
    for q in range(NB):
        rd=recip(a[q,q])
        c=[g(i,q) for i in range(NB)]
        t=[c[i]*rd for i in range(NB)]
        for i in range(NB):
            for j in range(i,NB):
                if i!=q and j!=q: a[i,j]=a[i,j]-c[i]*t[j]
        for i in range(NB):
            if i!=q: a[min(i,q),max(i,q)]=t[i]
        a[q,q]=-rd
    cols=[]
    for j in range(NB):
        v=g(0,j)
        for i in range(1,NB): v=jnp.where(sub==i,g(i,j),v)
        cols.append(-v)
    return cols
def tree(xs):
    while len(xs)>1: xs=[xs[i]+xs[i+1] if i+1<len(xs) else xs[i] for i in range(0,len(xs),2)]
    return xs[0]

def spd_inverse(G):
    n=128
    ri=lax.broadcasted_iota(jnp.int32,(n,n),0); ci=lax.broadcasted_iota(jnp.int32,(n,n),1)
    dg=jnp.where(ri==ci,G,0.0)
    sc=lax.rsqrt(jnp.sum(dg,axis=0,keepdims=True))*lax.rsqrt(jnp.sum(dg,axis=1,keepdims=True))
    A=G*sc
    lane=lax.broadcasted_iota(jnp.int32,(8,n),1); sub=lax.broadcasted_iota(jnp.int32,(8,n),0)
    rows=[A[8*i:8*i+8,:] for i in range(16)]
    nxt=rows[0]
    for p in range(16):
        k=8*p
        eye=(lane==sub+k).astype(F32)
        cols=block_cols(nxt,k,sub)
        R=nxt+eye
        W=tree([cols[j]*R[j:j+1,:] for j in range(NB)])
        wj=[W[j:j+1,:] for j in range(NB)]
        upd=lambda a: a-tree([a[:,k+j:k+j+1]*wj[j] for j in range(NB)])
        if p<15: nxt=upd(rows[p+1])
        rows=[W-eye if i==p else nxt if i==p+1 else upd(rows[i]) for i in range(16)]
    return jnp.concatenate(rows,0)*sc


def home(k):
    o=2*lax.rem(k,32)
    g=lax.rem(lax.div(k,32)+lax.rem(k,32)+lax.div(lax.rem(k,32),4)+lax.div(lax.rem(k,32),16),2)
    return g*64+o

def mega(t_hbm,o_hbm,p_hbm,ax_hbm,ay_hbm,wz_hbm,q_hbm,out,tc,ec,t_ref,vp,ax_ref,ay_ref,wz_ref,q_ref,xh,xl,part,gs,parts,sums,ub,ob,sb,kt,e,osend,arecv,brecv,crecv,drecv,tsend,trecv,esend,erecv,loc,tabs,rsend,rrecv,gsend,grecv,usend,urecv):
    g=lax.axis_index("grp"); o=lax.axis_index("orb"); me=g*64+o
    s=2*lax.rem(o,2)-1
    w=lambda v: lax.rem(v+128,64)
    inner=(g,w(o-s)); outer=(g,w(o+s)); across=(g,w(o-2*s))
    copies=[pltpu.make_async_copy(a,b,tabs.at[i]) for i,(a,b) in enumerate(((q_hbm,q_ref),(o_hbm,ob.at[0]),(t_hbm,t_ref),(ax_hbm,ax_ref),(ay_hbm,ay_ref),(wz_hbm,wz_ref),(p_hbm,vp)))]
    for c in copies: c.start()
    bar=pltpu.get_barrier_semaphore()
    def sig(k,c):
        pl.semaphore_signal(bar,inc=1,device_id=peer(lax.rem(me+k,NDEV)),device_id_type=MESH)
        return c
    lax.fori_loop(1,NDEV,sig,0)
    mask=lax.broadcasted_iota(jnp.int32,(32,128),1)<64
    copies[0].wait()
    qa=q_ref[0:64,:]
    def ktab(r,c):
        kt[pl.ds(pl.multiple_of(r*64,64),64),:]=(4*np.pi/CELLS)/(qa+q_ref[pl.ds(64+r,1),:])
        return c
    lax.fori_loop(0,32,ktab,0,unroll=8)
    for c in copies[1:]: c.wait()
    ax=ax_ref[...];ay=ay_ref[...];wz=wz_ref[...]
    o_ref=ob.at[0]
    def rows(q): return pl.ds(pl.multiple_of(q*CR,CR),CR)
    def fwd(j,q):
        pr=t_ref[rows(q),:]*ob[j,rows(q),:]
        b=[]
        for p in range(CP):
            b+=half_swap(pr[64*p:64*p+32],pr[64*p+32:64*p+64],mask)
        x=lanes(jnp.concatenate(b,0),wz)
        f=left(ay,[x[64*p:64*p+64] for p in range(CP)])
        out=[]
        for p in range(CP): out+=half_swap(f[p][:32],f[p][32:],mask)
        sb[j,rows(q),:]=jnp.concatenate(out,0)
    R=16
    def mid(j):
        def half(i,c):
            f=left(ax,[sb[j,pl.ds(i*R+r,64,stride=32),:] for r in range(R)])
            kk=kt[pl.ds(pl.multiple_of(i*R*64,R*64),R*64),:]
            f=left(ax,[f[r]*kk[64*r:64*r+64] for r in range(R)])
            for r in range(R): sb[j,pl.ds(i*R+r,64,stride=32),:]=f[r]
            return c
        lax.fori_loop(0,32//R,half,0)
    def inv(js,q,first):
        b=[]
        for j in js:
            sv=sb[j,rows(q),:]
            for p in range(CP):
                u,v=half_swap(sv[64*p:64*p+32],sv[64*p+32:64*p+64],mask)
                b.append(jnp.concatenate([u,v],0))
        x=lanes(jnp.concatenate(left(ay,b),0),wz)
        acc=None if first else e[rows(q),:]
        for n,j in enumerate(js):
            out=[]
            for p in range(CP):
                k=64*(n*CP+p)
                out+=half_swap(x[k:k+32],x[k+32:k+64],mask)
            term=jnp.concatenate(out,0)*ob[j,rows(q),:]
            acc=-term if acc is None else acc-term
        e[rows(q),:]=acc
    def chunks(f):
        def body(q,c):
            f(q)
            return c
        lax.fori_loop(0,CH,body,0)
    def push(dst_dev,slot,q,rsem,src):
        return pltpu.make_async_remote_copy(src_ref=src.at[rows(q),:],dst_ref=ob.at[slot,rows(q),:],send_sem=osend,recv_sem=rsem.at[q],device_id=dst_dev,device_id_type=MESH)
    def arrive(slot,q,rsem):
        pltpu.make_async_copy(ob.at[slot,rows(q),:],ob.at[slot,rows(q),:],rsem.at[q]).wait()
    chunks(lambda q: fwd(0,q))
    pl.semaphore_wait(bar,NDEV-1)
    def alone(v):
        c=lax.rem(lax.div(v,2),16)
        return ((c==3)|(c==12)).astype(jnp.int32)
    single=alone(o)
    def order(i,a=single):
        f=3*g*(1-a)
        return i+jnp.where(i==0,f,jnp.where(i==3,-f,0))
    f3=order(0)
    on_out,on_across=alone(w(o+s)),alone(w(o-2*s))
    twin=(1-g,o)
    def start_a(q): push(inner,1,q,arecv,o_ref).start()
    def loop(lo,hi,f):
        def body(i,c):
            f(i)
            return c
        lax.fori_loop(lo,hi,body,0)
    def start_bc(i):
        @pl.when(i<3+on_out)
        def _(): push(outer,2,order(i,on_out),brecv,o_ref).start()
        @pl.when(i<3+on_across)
        def _(): push(across,3,order(i,on_across),crecv,o_ref).start()
    loop(0,4,start_bc)
    chunks(start_a)
    def piece(buf,d):
        return buf.at[pl.ds(pl.multiple_of(lax.rem(d,64)*32+lax.div(d,64)*16,16),16),:]
    mine=pl.ds(pl.multiple_of(me*16,16),16)
    def t_send(k):
        d=lax.rem(me+45*k,NDEV)
        pltpu.make_async_remote_copy(src_ref=piece(t_ref,d),dst_ref=tc.at[mine,:],send_sem=tsend,recv_sem=trecv,device_id=peer(d),device_id_type=MESH).start()
    pltpu.make_async_copy(piece(t_ref,me),tc.at[mine,:],trecv).start()
    mid(0)
    chunks(lambda q: inv([0],q,True))
    def in_a(q):
        arrive(1,q,arecv)
        fwd(1,q)
    chunks(in_a)
    mid(1)
    arrive(2,f3,brecv)
    @pl.when(single==0)
    def _(): push(twin,2,f3,brecv,ob.at[2]).start()
    push(inner,4,f3,drecv,ob.at[2]).start()
    arrive(3,f3,crecv)
    @pl.when(single==0)
    def _(): push(twin,3,f3,crecv,ob.at[3]).start()
    chunks(lambda q: inv([1],q,False))
    def in_bcd(i):
        q=order(i)
        @pl.when(i>0)
        def _():
            arrive(2,q,brecv)
            push(inner,4,q,drecv,ob.at[2]).start()
        fwd(2,q)
        @pl.when(i>0)
        def _(): arrive(3,q,crecv)
        fwd(3,q)
        arrive(4,q,drecv)
        fwd(4,q)
    loop(0,3,in_bcd)
    loop(3,4,in_bcd)
    loop(1,NDEV,t_send)
    mid(2)
    mid(3)
    mid(4)
    def e_send(k,c):
        d=lax.rem(k,2)*64+lax.div(k,2)
        src=piece(e,d)
        @pl.when(d==me)
        def _(): pltpu.make_async_copy(src,ec.at[mine,:],erecv).start()
        @pl.when(d!=me)
        def _(): pltpu.make_async_remote_copy(src_ref=src,dst_ref=ec.at[mine,:],send_sem=esend,recv_sem=erecv,device_id=peer(d),device_id_type=MESH).start()
        return c
    def tail(q):
        inv([2,3,4],q,False)
        lax.fori_loop(q*4*CP,(q+1)*4*CP,e_send,0)
    chunks(tail)
    whole=lambda buf,n,sem: pltpu.make_async_copy(buf.at[pl.ds(0,n),:],buf.at[pl.ds(0,n),:],sem).wait()
    def spread(lo,hi):
        def send(n,c):
            src=part.at[pl.ds(pl.multiple_of(n*8,8),8),:]
            h=home(n)
            @pl.when(h==me)
            def _(): pltpu.make_async_copy(src,parts.at[me],rrecv).start()
            @pl.when(h!=me)
            def _(): pltpu.make_async_remote_copy(src_ref=src,dst_ref=parts.at[me],send_sem=rsend,recv_sem=rrecv,device_id=peer(h),device_id_type=MESH).start()
            return c
        lax.fori_loop(lo,hi,send,0)
    def nt(a,b): return lax.dot_general(a,b,(((1,),(1,)),((),())),preferred_element_type=F32)
    def rowset(buf,s): return buf[pl.ds(s,128,stride=16),:]
    def vrow(s): return vp[pl.ds(g*16+s,1),:]
    whole(tc,2048,trecv)
    for s in range(16):
        h,l=split(rowset(tc,s))
        xh[128:256,128*s:128*s+128]=h; xl[128:256,128*s:128*s+128]=l
        h,l=split(rowset(tc,s)*vrow(s))
        xh[0:128,128*s:128*s+128]=h; xl[0:128,128*s:128*s+128]=l
    part[256:384,:]=(nt(xh[0:128,:],xh[128:256,:])+nt(xh[0:128,:],xl[128:256,:])+nt(xl[0:128,:],xh[128:256,:]))*(1.0/CELLS)
    spread(32,48)
    whole(ec,2048,erecv)
    for s in range(16):
        h,l=split(rowset(ec,s))
        xh[0:128,128*s:128*s+128]=h; xl[0:128,128*s:128*s+128]=l
    part[0:256,:]=(nt(xh[...],xh[0:128,:])+nt(xh[...],xl[0:128,:])+nt(xl[...],xh[0:128,:]))*(1.0/CELLS)
    spread(0,32)
    def gather(n,c):
        @pl.when(home(n)==me)
        def _():
            pltpu.make_async_copy(parts,parts,rrecv).wait()
            sums[...]=jnp.sum(parts[...],axis=0)
            dst=gs.at[pl.ds(pl.multiple_of(n*8,8),8),:]
            pltpu.make_async_copy(sums,dst,grecv).start()
            def bc(j,c2):
                step=lambda v: jnp.where(v<2,2+v,3-v)
                dz,dy,dx=step(lax.div(j,32)),step(lax.rem(lax.div(j,8),4)),step(lax.rem(lax.div(j,2),4))
                y=lax.rem(2*lax.div(o,32)+g+dy,4)
                z=lax.rem(lax.div(o,8)+dz,4)
                x=lax.rem(lax.div(o,2)+dx,4)
                c=lax.rem(o+1+j,2)
                pltpu.make_async_remote_copy(src_ref=sums,dst_ref=dst,send_sem=gsend,recv_sem=grecv,device_id=(lax.rem(y,2),lax.div(y,2)*32+z*8+x*2+c),device_id_type=MESH).start()
                return c2
            lax.fori_loop(0,NDEV-1,bc,0)
        return c
    lax.fori_loop(0,48,gather,0)
    pltpu.make_async_copy(gs,gs,grecv).wait()
    HI=lax.Precision.HIGHEST
    def solve_small():
        gte=gs[128:256,:]
        m=jnp.dot(gte,spd_inverse(gs[0:128,:]),precision=HI,preferred_element_type=F32)
        sb[0,0:128,:]=m
        sb[0,128:256,:]=gs[256:384,:]-lax.dot_general(m,gte,(((1,),(1,)),((),())),precision=HI,preferred_element_type=F32)
    loop(0,1+lax.div(o,64),lambda i: solve_small())
    def coeff(which):
        b=which*64
        h0,l0=split(sb[0,pl.ds(pl.multiple_of(b,64),64),:]); h1,l1=split(sb[0,pl.ds(pl.multiple_of(128+b,64),64),:])
        return jnp.concatenate([h0,h1],1),jnp.concatenate([l0,l1],1)
    N=4
    def rows_of(which,i):
        h,l=coeff(which)
        c=pl.ds(pl.multiple_of(i*128*N,128*N),128*N)
        r=dot(h,xh[:,c])+dot(h,xl[:,c])+dot(l,xh[:,c])
        old=jnp.concatenate([tc[pl.ds(which*1024+i*N+n,64,stride=16),:] for n in range(N)],1)
        v=jnp.concatenate([vrow(i*N+n) for n in range(N)],1)
        return old-0.3*(v*old-r)
    other=1-g
    part_of=lambda base,i: pl.ds(pl.multiple_of(base+i*128*N,128*N),128*N)
    def swap_copy(i): return pltpu.make_async_remote_copy(src_ref=ub.at[:,part_of(0,i)],dst_ref=out.at[:,part_of(g*2048,i)],send_sem=usend.at[i],recv_sem=urecv.at[i],device_id=(other,o),device_id_type=MESH)
    def theirs(i):
        ub[:,part_of(0,i)]=rows_of(other,i)
        swap_copy(i).start()
    loop(0,16//N,theirs)
    def ours(i): out[:,part_of(g*2048,i)]=rows_of(g,i)
    loop(0,16//N,ours)
    def drain(n,c):
        @pl.when(home(n)!=me)
        def _(): pltpu.make_async_copy(sums,sums,rsend).wait()
        @pl.when(home(n)==me)
        def _(): pltpu.make_async_copy(parts.at[pl.ds(0,127)],parts.at[pl.ds(0,127)],gsend).wait()
        return c
    lax.fori_loop(0,48,drain,0)
    whole(tc,2032,tsend); whole(ec,2032,esend)
    def drain_occ(i,c):
        pltpu.make_async_copy(ob.at[0,rows(0),:],ob.at[0,rows(0),:],osend).wait()
        return c
    lax.fori_loop(0,16+on_out+on_across-2*single,drain_occ,0)
    for i in range(16//N): swap_copy(i).wait()

VM=pl.BlockSpec(memory_space=pltpu.VMEM)
ANY=pl.BlockSpec(memory_space=pl.ANY)
def mega_call(t,o,p):
    tabs=[jnp.asarray(a) for a in tables()]
    D=pltpu.SemaphoreType.DMA
    big=lambda *n: pltpu.VMEM(n+(2048,128),F32)
    return pl.pallas_call(mega,out_shape=jax.ShapeDtypeStruct((64,4096),F32),in_specs=[ANY]*7,out_specs=VM,
      scratch_shapes=[big(),big(),big(),pltpu.VMEM((32,128),F32),pltpu.VMEM((64,192),BF),pltpu.VMEM((64,192),BF),pltpu.VMEM((256,256),BF),pltpu.VMEM((96,128),F32),
        pltpu.VMEM((256,2048),BF),pltpu.VMEM((256,2048),BF),pltpu.VMEM((384,128),F32),pltpu.VMEM((384,128),F32),pltpu.VMEM((128,8,128),F32),pltpu.VMEM((8,128),F32),pltpu.VMEM((64,2048),F32),
        big(5),big(5),big(),big(),D,D((CH,)),D((CH,)),D((CH,)),D((CH,)),D,D,D,D,D,D((7,)),D,D,D,D,D((4,)),D((4,))],
      compiler_params=pltpu.CompilerParams(collective_id=0,has_side_effects=True,vmem_limit_bytes=58<<20))(t,o,p,*tabs)

def on_device(occupied, targets, potential):
    return mega_call(targets.reshape(2048, 128), occupied.reshape(2048, 128), potential.reshape(32, 128))


def solution(mesh):
    placed = (P("orb", None), P(("grp", "orb"), None), P("orb"))
    return jax.shard_map(
        on_device, mesh=mesh, in_specs=placed, out_specs=P("grp", "orb"), check_vma=False
    )
```

```python
import functools
import ml_dtypes
import jax
import jax.numpy as jnp
from jax.sharding import PartitionSpec as P
from jax import lax
from jax.experimental import pallas as pl
from jax.experimental.pallas import tpu as pltpu
import numpy as np
BF=jnp.bfloat16; F32=jnp.float32
MESH=pl.DeviceIdType.MESH
CELLS=262144
NDEV=128
CH=4
CP=32//CH
CR=2048//CH

def tables():
    bf=ml_dtypes.bfloat16
    i=np.arange(64)
    ang=2*np.pi*((i[:,None]*i[None,:])%64)/64
    H=(np.cos(ang)+np.sin(ang)).astype(np.float32)
    Hh=H.astype(bf); Hl=(H-Hh.astype(np.float32)).astype(bf)
    perm=2*(i%32)+i//32
    ax=np.concatenate([Hh,Hh,Hl],1)
    ay=ax.reshape(64,3,64)[perm][:,:,perm].reshape(64,192)
    z=np.zeros((64,64),bf)
    bd=lambda m: np.block([[m,z],[z,m]])
    row=np.concatenate([bd(Hh),bd(Hl)],1)
    wz=np.concatenate([row,row],0)
    q=np.minimum(i,64-i).astype(np.float32)*np.float32(2*np.pi/20.0); q2=q*q
    qa=np.broadcast_to((q2+np.float32(0.04))[:,None],(64,128))
    qb=q2.reshape(32,2)
    qr=(qb[:,:,None]+q2[None,None,:]).reshape(32,128)
    return ax,ay,wz,np.concatenate([qa,qr],0).astype(np.float32)

def split(x):
    h=x.astype(BF)
    return h,(x-h.astype(F32)).astype(BF)
def dot(a,b): return jnp.dot(a,b,preferred_element_type=F32)
def half_swap(lo,hi,mask):
    return jnp.where(mask,lo,pltpu.roll(hi,64,1)), jnp.where(mask,pltpu.roll(lo,64,1),hi)
def left(A,planes):
    out=[]
    for k in range(0,len(planes),2):
        h,l=split(jnp.concatenate(planes[k:k+2],1))
        r=dot(A,jnp.concatenate([h,l,h],0))
        out+=[r[:,:128],r[:,128:]]
    return out
def lanes(x,W):
    h,l=split(x)
    r=dot(jnp.concatenate([h,l],1),W)
    return r[:,:128]+r[:,128:]

def peer(d): return (lax.div(d,64),lax.rem(d,64))

NB=8
def recip(x):
    y=pl.reciprocal(x,approx=True)
    y=y*(2.0-x*y)
    return y*(2.0-x*y)
def block_cols(Bp,k,sub):
    a={}
    for i in range(NB):
        for j in range(i,NB):
            a[i,j]=jnp.broadcast_to(Bp[i:i+1,k+j:k+j+1],(NB,128))
    g=lambda i,j: a[min(i,j),max(i,j)]
    for q in range(NB):
        rd=recip(a[q,q])
        c=[g(i,q) for i in range(NB)]
        t=[c[i]*rd for i in range(NB)]
        for i in range(NB):
            for j in range(i,NB):
                if i!=q and j!=q: a[i,j]=a[i,j]-c[i]*t[j]
        for i in range(NB):
            if i!=q: a[min(i,q),max(i,q)]=t[i]
        a[q,q]=-rd
    cols=[]
    for j in range(NB):
        v=g(0,j)
        for i in range(1,NB): v=jnp.where(sub==i,g(i,j),v)
        cols.append(-v)
    return cols
def tree(xs):
    while len(xs)>1: xs=[xs[i]+xs[i+1] if i+1<len(xs) else xs[i] for i in range(0,len(xs),2)]
    return xs[0]

def spd_inverse(G):
    n=128
    ri=lax.broadcasted_iota(jnp.int32,(n,n),0); ci=lax.broadcasted_iota(jnp.int32,(n,n),1)
    dg=jnp.where(ri==ci,G,0.0)
    sc=lax.rsqrt(jnp.sum(dg,axis=0,keepdims=True))*lax.rsqrt(jnp.sum(dg,axis=1,keepdims=True))
    A=G*sc
    lane=lax.broadcasted_iota(jnp.int32,(8,n),1); sub=lax.broadcasted_iota(jnp.int32,(8,n),0)
    rows=[A[8*i:8*i+8,:] for i in range(16)]
    nxt=rows[0]
    for p in range(16):
        k=8*p
        eye=(lane==sub+k).astype(F32)
        cols=block_cols(nxt,k,sub)
        R=nxt+eye
        W=tree([cols[j]*R[j:j+1,:] for j in range(NB)])
        wj=[W[j:j+1,:] for j in range(NB)]
        upd=lambda a: a-tree([a[:,k+j:k+j+1]*wj[j] for j in range(NB)])
        if p<15: nxt=upd(rows[p+1])
        rows=[W-eye if i==p else nxt if i==p+1 else upd(rows[i]) for i in range(16)]
    return jnp.concatenate(rows,0)*sc


def home(k):
    o=2*lax.rem(k,32)
    g=lax.rem(lax.div(k,32)+lax.rem(k,32)+lax.div(lax.rem(k,32),4)+lax.div(lax.rem(k,32),16),2)
    return g*64+o

def mega(t_hbm,o_hbm,p_hbm,ax_hbm,ay_hbm,wz_hbm,q_hbm,out,tc,ec,t_ref,vp,ax_ref,ay_ref,wz_ref,q_ref,xh,xl,part,gs,parts,sums,ub,ub2,ob,sb,kt,e,osend,arecv,brecv,crecv,drecv,tsend,trecv,esend,erecv,loc,tabs,rsend,rrecv,gsend,grecv,usend,urecv,ksem):
    g=lax.axis_index("grp"); o=lax.axis_index("orb"); me=g*64+o
    s=2*lax.rem(o,2)-1
    w=lambda v: lax.rem(v+128,64)
    inner=(g,w(o-s)); outer=(g,w(o+s)); across=(g,w(o-2*s))
    copies=[pltpu.make_async_copy(a,b,tabs.at[i]) for i,(a,b) in enumerate(((q_hbm,q_ref),(o_hbm,ob.at[0]),(t_hbm,t_ref),(ax_hbm,ax_ref),(ay_hbm,ay_ref),(wz_hbm,wz_ref),(p_hbm,vp)))]
    for c in copies: c.start()
    bar=pltpu.get_barrier_semaphore()
    def sig(k,c):
        pl.semaphore_signal(bar,inc=1,device_id=peer(lax.rem(me+k,NDEV)),device_id_type=MESH)
        return c
    lax.fori_loop(1,NDEV,sig,0)
    mask=lax.broadcasted_iota(jnp.int32,(32,128),1)<64
    copies[0].wait()
    qa=q_ref[0:64,:]
    def ktab(r,c):
        kt[pl.ds(pl.multiple_of(r*64,64),64),:]=(4*np.pi/CELLS)/(qa+q_ref[pl.ds(64+r,1),:])
        return c
    lax.fori_loop(0,32,ktab,0,unroll=8)
    for c in copies[1:]: c.wait()
    ax=ax_ref[...];ay=ay_ref[...];wz=wz_ref[...]
    o_ref=ob.at[0]
    def rows(q): return pl.ds(pl.multiple_of(q*CR,CR),CR)
    def fwd(j,q):
        pr=t_ref[rows(q),:]*ob[j,rows(q),:]
        b=[]
        for p in range(CP):
            b+=half_swap(pr[64*p:64*p+32],pr[64*p+32:64*p+64],mask)
        x=lanes(jnp.concatenate(b,0),wz)
        f=left(ay,[x[64*p:64*p+64] for p in range(CP)])
        out=[]
        for p in range(CP): out+=half_swap(f[p][:32],f[p][32:],mask)
        sb[j,rows(q),:]=jnp.concatenate(out,0)
    R=16
    def mid(j):
        def half(i,c):
            f=left(ax,[sb[j,pl.ds(i*R+r,64,stride=32),:] for r in range(R)])
            kk=kt[pl.ds(pl.multiple_of(i*R*64,R*64),R*64),:]
            f=left(ax,[f[r]*kk[64*r:64*r+64] for r in range(R)])
            for r in range(R): sb[j,pl.ds(i*R+r,64,stride=32),:]=f[r]
            return c
        lax.fori_loop(0,32//R,half,0)
    def inv(js,q,first):
        b=[]
        for j in js:
            sv=sb[j,rows(q),:]
            for p in range(CP):
                u,v=half_swap(sv[64*p:64*p+32],sv[64*p+32:64*p+64],mask)
                b.append(jnp.concatenate([u,v],0))
        x=lanes(jnp.concatenate(left(ay,b),0),wz)
        acc=None if first else e[rows(q),:]
        for n,j in enumerate(js):
            out=[]
            for p in range(CP):
                k=64*(n*CP+p)
                out+=half_swap(x[k:k+32],x[k+32:k+64],mask)
            term=jnp.concatenate(out,0)*ob[j,rows(q),:]
            acc=-term if acc is None else acc-term
        e[rows(q),:]=acc
    def chunks(f):
        def body(q,c):
            f(q)
            return c
        lax.fori_loop(0,CH,body,0)
    def push(dst_dev,slot,q,rsem,src):
        return pltpu.make_async_remote_copy(src_ref=src.at[rows(q),:],dst_ref=ob.at[slot,rows(q),:],send_sem=osend,recv_sem=rsem.at[q],device_id=dst_dev,device_id_type=MESH)
    def arrive(slot,q,rsem):
        pltpu.make_async_copy(ob.at[slot,rows(q),:],ob.at[slot,rows(q),:],rsem.at[q]).wait()
    chunks(lambda q: fwd(0,q))
    pl.semaphore_wait(bar,NDEV-1)
    def alone(v):
        c=lax.rem(lax.div(v,2),16)
        return ((c==3)|(c==12)).astype(jnp.int32)
    single=alone(o)
    def order(i,a=single):
        f=3*g*(1-a)
        return i+jnp.where(i==0,f,jnp.where(i==3,-f,0))
    f3=order(0)
    on_out,on_across=alone(w(o+s)),alone(w(o-2*s))
    twin=(1-g,o)
    def start_a(q): push(inner,1,q,arecv,o_ref).start()
    def loop(lo,hi,f):
        def body(i,c):
            f(i)
            return c
        lax.fori_loop(lo,hi,body,0)
    def start_bc(i):
        @pl.when(i<3+on_out)
        def _(): push(outer,2,order(i,on_out),brecv,o_ref).start()
        @pl.when(i<3+on_across)
        def _(): push(across,3,order(i,on_across),crecv,o_ref).start()
    loop(0,4,start_bc)
    chunks(start_a)
    def piece(buf,d):
        return buf.at[pl.ds(pl.multiple_of(lax.rem(d,64)*32+lax.div(d,64)*16,16),16),:]
    mine=pl.ds(pl.multiple_of(me*16,16),16)
    def t_send(k):
        d=lax.rem(me+45*k,NDEV)
        pltpu.make_async_remote_copy(src_ref=piece(t_ref,d),dst_ref=tc.at[mine,:],send_sem=tsend,recv_sem=trecv,device_id=peer(d),device_id_type=MESH).start()
    pltpu.make_async_copy(piece(t_ref,me),tc.at[mine,:],trecv).start()
    mid(0)
    chunks(lambda q: inv([0],q,True))
    def in_a(q):
        arrive(1,q,arecv)
        fwd(1,q)
    chunks(in_a)
    mid(1)
    arrive(2,f3,brecv)
    @pl.when(single==0)
    def _(): push(twin,2,f3,brecv,ob.at[2]).start()
    push(inner,4,f3,drecv,ob.at[2]).start()
    arrive(3,f3,crecv)
    @pl.when(single==0)
    def _(): push(twin,3,f3,crecv,ob.at[3]).start()
    chunks(lambda q: inv([1],q,False))
    def in_bcd(i):
        q=order(i)
        @pl.when(i>0)
        def _():
            arrive(2,q,brecv)
            push(inner,4,q,drecv,ob.at[2]).start()
        fwd(2,q)
        @pl.when(i>0)
        def _(): arrive(3,q,crecv)
        fwd(3,q)
        arrive(4,q,drecv)
        fwd(4,q)
    loop(0,3,in_bcd)
    loop(3,4,in_bcd)
    loop(1,NDEV,t_send)
    mid(2)
    mid(3)
    mid(4)
    def e_send(q,k,c):
        n=q*4*CP+lax.rem(k+5*me,4*CP)
        d=lax.rem(n,2)*64+lax.div(n,2)
        src=piece(e,d)
        @pl.when(d==me)
        def _(): pltpu.make_async_copy(src,ec.at[mine,:],erecv).start()
        @pl.when(d!=me)
        def _(): pltpu.make_async_remote_copy(src_ref=src,dst_ref=ec.at[mine,:],send_sem=esend,recv_sem=erecv,device_id=peer(d),device_id_type=MESH).start()
        return c
    def tail(i):
        q=lax.rem(i+lax.div(o,2),CH)
        inv([2,3,4],q,False)
        lax.fori_loop(0,4*CP,functools.partial(e_send,q),0)
    chunks(tail)
    whole=lambda buf,n,sem: pltpu.make_async_copy(buf.at[pl.ds(0,n),:],buf.at[pl.ds(0,n),:],sem).wait()
    def spread(lo,hi):
        def send(k,c):
            n=lo+lax.rem(k+me,hi-lo)
            src=part.at[pl.ds(pl.multiple_of(n*8,8),8),:]
            h=home(n)
            @pl.when(h==me)
            def _(): pltpu.make_async_copy(src,parts.at[me],rrecv).start()
            @pl.when(h!=me)
            def _(): pltpu.make_async_remote_copy(src_ref=src,dst_ref=parts.at[me],send_sem=rsend,recv_sem=rrecv,device_id=peer(h),device_id_type=MESH).start()
            return c
        lax.fori_loop(0,hi-lo,send,0)
    def nt(a,b): return lax.dot_general(a,b,(((1,),(1,)),((),())),preferred_element_type=F32)
    def rowset(buf,s): return buf[pl.ds(s,128,stride=16),:]
    def vrow(s): return vp[pl.ds(g*16+s,1),:]
    whole(tc,2048,trecv)
    for s in range(16):
        h,l=split(rowset(tc,s))
        xh[128:256,128*s:128*s+128]=h; xl[128:256,128*s:128*s+128]=l
        h,l=split(rowset(tc,s)*vrow(s))
        xh[0:128,128*s:128*s+128]=h; xl[0:128,128*s:128*s+128]=l
    part[256:384,:]=(nt(xh[0:128,:],xh[128:256,:])+nt(xh[0:128,:],xl[128:256,:])+nt(xl[0:128,:],xh[128:256,:]))*(1.0/CELLS)
    spread(32,48)
    whole(ec,2048,erecv)
    for s in range(16):
        h,l=split(rowset(ec,s))
        xh[0:128,128*s:128*s+128]=h; xl[0:128,128*s:128*s+128]=l
    def gram_rows(a):
        part[a:a+128,:]=(nt(xh[a:a+128,:],xh[0:128,:])+nt(xh[a:a+128,:],xl[0:128,:])+nt(xl[a:a+128,:],xh[0:128,:]))*(1.0/CELLS)
    gram_rows(0)
    spread(0,16)
    gram_rows(128)
    spread(16,32)
    line=[lax.rem(lax.div(o,2)+dx,4)*2+lax.rem(o+dc,2) for dx in (2,3,1,0) for dc in (1,0)]
    def gather(n,c):
        @pl.when(home(n)==me)
        def _():
            pltpu.make_async_copy(parts,parts,rrecv).wait()
            sums[...]=jnp.sum(parts[...],axis=0)
            dst=gs.at[pl.ds(pl.multiple_of(n*8,8),8),:]
            late=(n>=16).astype(jnp.int32)
            pltpu.make_async_copy(sums,dst,grecv.at[late]).start()
            def bc(j,c2):
                step=lambda v: jnp.where(v<2,2+v,3-v)
                y=lax.rem(2*lax.div(o,32)+g+step(lax.rem(j,4)),4)
                z=lax.rem(lax.div(o,8)+step(lax.div(j,4)),4)
                row,base=lax.rem(y,2),lax.div(y,2)*32+z*8
                def go(v): pltpu.make_async_remote_copy(src_ref=sums,dst_ref=dst,send_sem=gsend,recv_sem=grecv.at[late],device_id=(row,base+v),device_id_type=MESH).start()
                for v in line[:-1]: go(v)
                @pl.when(j<15)
                def _(): go(line[-1])
                return c2
            lax.fori_loop(0,16,bc,0)
        return c
    lax.fori_loop(0,48,gather,0)
    def summed(a,b,i): pltpu.make_async_copy(gs.at[a:b,:],gs.at[a:b,:],grecv.at[i]).wait()
    summed(0,128,0)
    HI=lax.Precision.HIGHEST
    def solve_small():
        sb[0,256:384,:]=spd_inverse(gs[0:128,:])
    def combine():
        gte=gs[128:256,:]
        m=jnp.dot(gte,sb[0,256:384,:],precision=HI,preferred_element_type=F32)
        sb[0,0:128,:]=m
        sb[0,128:256,:]=gs[256:384,:]-lax.dot_general(m,gte,(((1,),(1,)),((),())),precision=HI,preferred_element_type=F32)
    loop(0,1+lax.div(o,64),lambda i: solve_small())
    summed(128,384,1)
    loop(0,1+lax.div(o,64),lambda i: combine())
    def coeff(which):
        b=which*64
        h0,l0=split(sb[0,pl.ds(pl.multiple_of(b,64),64),:]); h1,l1=split(sb[0,pl.ds(pl.multiple_of(128+b,64),64),:])
        return jnp.concatenate([h0,h1],1),jnp.concatenate([l0,l1],1)
    N=4
    def rows_of(which,i):
        h,l=coeff(which)
        c=pl.ds(pl.multiple_of(i*128*N,128*N),128*N)
        r=dot(h,xh[:,c])+dot(h,xl[:,c])+dot(l,xh[:,c])
        old=jnp.concatenate([tc[pl.ds(which*1024+i*N+n,64,stride=16),:] for n in range(N)],1)
        v=jnp.concatenate([vrow(i*N+n) for n in range(N)],1)
        return old-0.3*(v*old-r)
    other=1-g
    part_of=lambda base,i: pl.ds(pl.multiple_of(base+i*128*N,128*N),128*N)
    def swap_copy(i): return pltpu.make_async_remote_copy(src_ref=ub.at[:,part_of(0,i)],dst_ref=out.at[:,part_of(g*2048,i)],send_sem=usend.at[i],recv_sem=urecv.at[i],device_id=(other,o),device_id_type=MESH)
    def theirs(i):
        ub[:,part_of(0,i)]=rows_of(other,i)
        swap_copy(i).start()
    loop(0,16//N,theirs)
    def keep(i): return pltpu.make_async_copy(ub2.at[:,part_of(0,i)],out.at[:,part_of(g*2048,i)],ksem.at[i])
    def ours(i):
        ub2[:,part_of(0,i)]=rows_of(g,i)
        keep(i).start()
    loop(0,16//N,ours)
    def drain(n,c):
        @pl.when(home(n)!=me)
        def _(): pltpu.make_async_copy(sums,sums,rsend).wait()
        @pl.when(home(n)==me)
        def _(): pltpu.make_async_copy(parts.at[pl.ds(0,127)],parts.at[pl.ds(0,127)],gsend).wait()
        return c
    lax.fori_loop(0,48,drain,0)
    whole(tc,2032,tsend); whole(ec,2032,esend)
    def drain_occ(i,c):
        pltpu.make_async_copy(ob.at[0,rows(0),:],ob.at[0,rows(0),:],osend).wait()
        return c
    lax.fori_loop(0,16+on_out+on_across-2*single,drain_occ,0)
    for i in range(16//N): keep(i).wait()
    for i in range(16//N): swap_copy(i).wait()

VM=pl.BlockSpec(memory_space=pltpu.VMEM)
ANY=pl.BlockSpec(memory_space=pl.ANY)
def mega_call(t,o,p):
    tabs=[jnp.asarray(a) for a in tables()]
    D=pltpu.SemaphoreType.DMA
    big=lambda *n: pltpu.VMEM(n+(2048,128),F32)
    return pl.pallas_call(mega,out_shape=jax.ShapeDtypeStruct((64,4096),F32),in_specs=[ANY]*7,out_specs=ANY,
      scratch_shapes=[big(),big(),big(),pltpu.VMEM((32,128),F32),pltpu.VMEM((64,192),BF),pltpu.VMEM((64,192),BF),pltpu.VMEM((256,256),BF),pltpu.VMEM((96,128),F32),
        pltpu.VMEM((256,2048),BF),pltpu.VMEM((256,2048),BF),pltpu.VMEM((384,128),F32),pltpu.VMEM((384,128),F32),pltpu.VMEM((128,8,128),F32),pltpu.VMEM((8,128),F32),pltpu.VMEM((64,2048),F32),pltpu.VMEM((64,2048),F32),
        big(5),big(5),big(),big(),D,D((CH,)),D((CH,)),D((CH,)),D((CH,)),D,D,D,D,D,D((7,)),D,D,D,D((2,)),D((4,)),D((4,)),D((4,))],
      compiler_params=pltpu.CompilerParams(collective_id=0,has_side_effects=True,vmem_limit_bytes=58<<20))(t,o,p,*tabs)

def on_device(occupied, targets, potential):
    return mega_call(targets.reshape(2048, 128), occupied.reshape(2048, 128), potential.reshape(32, 128))


def solution(mesh):
    placed = (P("orb", None), P(("grp", "orb"), None), P("orb"))
    return jax.shard_map(
        on_device, mesh=mesh, in_specs=placed, out_specs=P("grp", "orb"), check_vma=False
    )
```
